128 devices in a mesh: front: 4 (over y), row: 8 (over z, x_lo), col: 4 (over x_hi, core).
Axes of the slice: x: 4 (x_hi: 2, x_lo: 2; x = x_hi * 2 + x_lo), y: 4, z: 4, core: 2. Of those that a mesh axis runs over, the one named last changes fastest.
Arguments:
- front_entries: bfloat16 [36864, 9216], P(('front', 'row'), 'col'), parts along dimension 0, as said below
- children: bfloat16 [8, 8192, 8192], P('front', 'row', 'col'), parts along dimension 0, as said below
- child_maps: int32 [8, 64], P('front'), parts along dimension 0, may hold values from 0 to 71, as said below
Outputs:
- factor: float32 [36864, 9216], P(('front', 'row'), 'col'), parts along dimension 0
The draws below stay inside these ranges and needn't reach their ends.
There are 4 independent parts, one for each index of `front`. The reference program is written for one: setup_inputs(seed, part) draws one part's arguments, and reference() takes and returns one part's arrays. A program takes and returns all parts, laid end to end along the dimension named above; each array names one. Nothing has to cross between parts.
Inputs may be any that keep to these rules, and one draw needn't show every extreme that they name: `front_entries`: symmetric in natural order; the leading 256 x 256 block of the matrix assembled by the steps is positive definite. `children`: each child's matrix is symmetric in natural order. `child_maps`: the entries of one child are distinct. For each child, among its blocks k with k mod 8 = a, exactly 1 has a value v with v mod 8 = d, for every a and d; and among its blocks k with k mod 4 = a, exactly 4 have a value v with v mod 4 = d, for every a and d.
All inputs are finite; a program needn't handle non-finite values.
Results may differ from the reference program's by a relative error of at most 0.0003.
Values may be sent and summed in bfloat16 or wider, within the bound.
A program may use at most 128 MiB of HBM per device.

```python
import math
import jax
import jax.numpy as jnp
from jax import lax

NP = 9216
CH = 8192
BLK = 128
SEP = 256
N_ROW = 8
N_COL = 4


def natural_index_drawn(length, pieces):
    stored = jnp.arange(length, dtype=jnp.int32)
    per_device = length // pieces
    device = stored // per_device
    within = stored % per_device
    return (within // BLK * pieces + device) * BLK + within % BLK


def symmetric_noise(noise_key, shape):
    raw = jnp.clip(jax.random.normal(noise_key, shape, jnp.float32), -4.0, 4.0)
    return (raw + jnp.swapaxes(raw, -1, -2)) * (0.5 * math.sqrt(0.5))


def draw_front_entries(key, part):
    base_key = jax.random.fold_in(key, 11)
    key_noise, key_lead, key_rest = jax.random.split(base_key, 3)
    noise = symmetric_noise(key_noise, (NP, NP))
    places = jnp.arange(NP)
    leading = places < SEP
    coupling = leading[:, None] != leading[None, :]
    noise = jnp.where(coupling, 4.0 * noise, noise)
    lead_diagonal = jax.random.uniform(key_lead, (NP,), jnp.float32, 1.5, 2.5) * (1.75 * math.sqrt(SEP))
    rest_diagonal = jax.random.uniform(key_rest, (NP,), jnp.float32, 0.5, 2.0)
    diagonal = jnp.where(leading, lead_diagonal, rest_diagonal)
    whole = jnp.where(places[:, None] == places[None, :], diagonal[:, None], noise)
    row_index = natural_index_drawn(NP, N_ROW)
    col_index = natural_index_drawn(NP, N_COL)
    return whole[row_index[:, None], col_index[None, :]].astype(jnp.bfloat16)


def draw_children(key, part):
    base_key = jax.random.fold_in(key, 23)
    noise = symmetric_noise(base_key, (2, CH, CH))
    row_index = natural_index_drawn(CH, N_ROW)
    col_index = natural_index_drawn(CH, N_COL)
    return noise[:, row_index[:, None], col_index[None, :]].astype(jnp.bfloat16)


def one_map(map_key, period, steps, slots):
    key_shift, key_slot = jax.random.split(map_key)
    shifts = jax.random.permutation(key_shift, period)
    block_ids = jnp.arange(steps)
    sources = jnp.arange(period)
    residue = (sources[None, :] + shifts[block_ids % period][:, None]) % period
    tables = jax.vmap(lambda subkey: jax.random.permutation(subkey, slots))(jax.random.split(key_slot, period))
    tables = (tables - tables[:, :1] + slots - 1) % slots
    chosen = tables[residue, block_ids[:, None]]
    return (chosen * period + residue).reshape(-1).astype(jnp.int32)


def draw_child_maps(key, part):
    base_key = jax.random.fold_in(key, 37)
    period = max(N_ROW, N_COL)
    steps = CH // BLK // period
    slots = NP // BLK // period
    both_keys = jax.random.split(base_key, 2)
    return jnp.stack([one_map(both_keys[0], period, steps, slots), one_map(both_keys[1], period, steps, slots)])


def setup_inputs(seed: int = 0, part: int = 0) -> dict:
    key_of = jax.random.split(jax.random.key(seed), 4)
    own_keys = jax.random.split(jax.random.fold_in(key_of[3], part), 4)
    return {
        "front_entries": draw_front_entries(jax.random.fold_in(jax.random.fold_in(key_of[3], part), 71), part),
        "children": draw_children(jax.random.fold_in(jax.random.fold_in(key_of[3], part), 71), part),
        "child_maps": draw_child_maps(jax.random.fold_in(jax.random.fold_in(key_of[3], part), 71), part),
    }


def natural_index(length, pieces):
    stored = jnp.arange(length, dtype=jnp.int32)
    per_device = length // pieces
    device = stored // per_device
    within = stored % per_device
    return ((within // BLK * pieces + device) * BLK + within % BLK).astype(jnp.int32)

def reference(front_entries, children, child_maps):
    row_index = natural_index(NP, N_ROW)
    col_index = natural_index(NP, N_COL)
    assembled = jnp.zeros((NP, NP), jnp.float32)
    assembled = assembled.at[row_index[:, None], col_index[None, :]].set(front_entries.astype(jnp.float32))
    child_rows = natural_index(CH, N_ROW)
    child_cols = natural_index(CH, N_COL)
    for child_index in range(2):
        spread_map = child_maps[child_index]
        dest_rows = (spread_map[child_rows // BLK] * BLK + child_rows % BLK).astype(jnp.int32)
        dest_cols = (spread_map[child_cols // BLK] * BLK + child_cols % BLK).astype(jnp.int32)
        assembled = assembled.at[dest_rows[:, None], dest_cols[None, :]].add(children[child_index].astype(jnp.float32))
    corner = jnp.tril(jnp.linalg.cholesky(assembled[:SEP, :SEP]))
    panel = lax.linalg.triangular_solve(corner, assembled[SEP:, :SEP], left_side=False, lower=True, transpose_a=True)
    schur_part = assembled[SEP:, SEP:] - jnp.dot(panel.astype(jnp.float32), panel.T.astype(jnp.float32), precision=lax.Precision.HIGHEST, preferred_element_type=jnp.float32)
    top_half = jnp.concatenate([corner, jnp.zeros((SEP, NP - SEP), jnp.float32)], axis=1)
    bottom = jnp.concatenate([panel, schur_part], axis=1)
    natural = jnp.concatenate([top_half, bottom], axis=0)
    return natural[row_index[:, None], col_index[None, :]]
```

```python
import jax
import jax.numpy as jnp
from jax import lax
from jax.experimental import pallas as pl
from jax.experimental.pallas import tpu as pltpu
from jax.sharding import PartitionSpec as P

BLK = 128
F32 = jnp.float32
BF16 = jnp.bfloat16
HIGH = lax.Precision.HIGHEST


def pack_kernel(maps, pos, children, out, buf, packed, row_of, col_of, in_sem, out_sem):
    own_row, own_col = pos[0], pos[1]
    for c in range(2):
        for k in range(8):
            row_of[c, maps[c, k * 8 + own_row] % 8] = k
        for k in range(16):
            col_of[c, (k % 2) * 8 + maps[c, k * 4 + own_col] % 8] = k
    for d in range(8):
        for c in range(2):
            pltpu.make_async_copy(
                children.at[c, pl.ds(row_of[c, d] * BLK, BLK), :], buf.at[d, c], in_sem.at[d]
            ).start()

    def one_row(d, carry):
        for c in range(2):
            pltpu.make_async_copy(children.at[0, pl.ds(0, BLK), :], buf.at[d, c], in_sem.at[d]).wait()
        for c in range(2):
            for half in range(2):
                for delta in range(8):
                    start = pl.multiple_of(col_of[c, half * 8 + delta] * BLK, BLK)
                    packed[d, delta % 4, half, delta // 4, c] = buf[d, c, :, pl.ds(start, BLK)]
        pltpu.make_async_copy(packed.at[d], out.at[d], out_sem.at[0]).start()
        return carry

    lax.fori_loop(0, 8, one_row, 0)
    pltpu.make_async_copy(packed, out, out_sem.at[0]).wait()


def pack(children, child_maps, pos):
    return pl.pallas_call(
        pack_kernel,
        out_shape=jax.ShapeDtypeStruct((8, 4, 2, 2, 2, BLK, BLK), BF16),
        in_specs=[
            pl.BlockSpec(memory_space=pltpu.SMEM),
            pl.BlockSpec(memory_space=pltpu.SMEM),
            pl.BlockSpec(memory_space=pl.ANY),
        ],
        out_specs=pl.BlockSpec(memory_space=pl.ANY),
        scratch_shapes=[
            pltpu.VMEM((8, 2, BLK, 16 * BLK), BF16),
            pltpu.VMEM((8, 4, 2, 2, 2, BLK, BLK), BF16),
            pltpu.SMEM((2, 8), jnp.int32),
            pltpu.SMEM((2, 16), jnp.int32),
            pltpu.SemaphoreType.DMA((8,)),
            pltpu.SemaphoreType.DMA((1,)),
        ],
        compiler_params=pltpu.CompilerParams(vmem_limit_bytes=40 << 20),
        name="pack",
    )(child_maps, pos, children)


def slot_tables(child_maps, own_row, own_col):
    ids = jnp.arange(64, dtype=jnp.int32)
    rows = jnp.arange(9, dtype=jnp.int32) * 8 + own_row
    cols = jnp.arange(18, dtype=jnp.int32) * 4 + own_col
    unit = ids % 4 * 2 + ids % 8 // 4
    row_tab = jnp.max(jnp.where(child_maps[:, None, :] == rows[None, :, None], ids % 8, -1), axis=2)
    col_tab = jnp.max(jnp.where(child_maps[:, None, :] == cols[None, :, None], unit, -1), axis=2)
    return jnp.concatenate([row_tab, col_tab], axis=1).astype(jnp.int32)


def panel_kernel(tab, recv, front, out, acc, sem):
    out[...] = front[...].astype(F32)
    for c in range(2):
        col = tab[c, 9]
        for s in range(9):
            row = tab[c, s]

            @pl.when((row >= 0) & (col >= 0))
            def _():
                copy = pltpu.make_async_copy(recv.at[row, col, 0, c], acc, sem)
                copy.start()
                copy.wait()
                out[pl.ds(s * BLK, BLK), :] += acc[...].astype(F32)


def panel(recv, front, tab):
    return pl.pallas_call(
        panel_kernel,
        out_shape=jax.ShapeDtypeStruct((9 * BLK, BLK), F32),
        grid=(1,),
        in_specs=[
            pl.BlockSpec(memory_space=pltpu.SMEM),
            pl.BlockSpec(memory_space=pl.ANY),
            pl.BlockSpec((9 * BLK, BLK), lambda i: (0, 0)),
        ],
        out_specs=pl.BlockSpec((9 * BLK, BLK), lambda i: (0, 0)),
        scratch_shapes=[pltpu.VMEM((BLK, BLK), BF16), pltpu.SemaphoreType.DMA(())],
        name="panel",
    )(tab, recv, front)


def split(x):
    hi = x.astype(BF16)
    lo = (x - hi.astype(F32)).astype(BF16)
    return hi, lo


def final_kernel(tab, pos, recv0, recv1, front, rows, cols, out, colcat):
    s = pl.program_id(0)
    own_row, own_col = pos[0], pos[1]

    @pl.when(s == 0)
    def _():
        hi, lo = split(cols[...])
        colcat[:, pl.ds(0, 256)] = hi
        colcat[:, pl.ds(256, 256)] = lo

    lead = (s == 0) & (own_row < 2)

    @pl.when(lead)
    def _():
        out[...] = jnp.zeros_like(out)

        @pl.when(own_col < 2)
        def _():
            r = lax.broadcasted_iota(jnp.int32, (BLK, BLK), 0) + own_row * BLK
            k = lax.broadcasted_iota(jnp.int32, (BLK, BLK), 1) + own_col * BLK
            mine = jnp.where(own_col == 0, rows[:, pl.ds(0, BLK)], rows[:, pl.ds(BLK, BLK)])
            out[:, pl.ds(0, BLK)] = jnp.where(r >= k, mine, 0.0)

    @pl.when(jnp.logical_not(lead))
    def _():
        hi, lo = split(rows[...])
        left = jnp.concatenate([hi, lo, hi], axis=1)
        for t in range(18):
            part = pl.ds(t * BLK, BLK)
            right = jnp.concatenate(
                [colcat[part, pl.ds(0, 256)], colcat[part, pl.ds(0, 256)], colcat[part, pl.ds(256, 256)]], axis=1
            )
            val = front[:, part].astype(F32) - lax.dot_general(
                left, right, (((1,), (1,)), ((), ())), preferred_element_type=F32
            )
            for c, recv in enumerate((recv0, recv1)):
                u = tab[c, 9 + t]
                ok = (u >= 0) & (tab[c, s] >= 0)
                blk = recv[0, jnp.maximum(u, 0), t % 2, 0].astype(F32)
                val += jnp.where(ok, blk, 0.0)
            out[:, part] = val

        @pl.when(own_col < 2)
        def _():
            out[:, pl.ds(0, BLK)] = jnp.where(own_col == 0, rows[:, pl.ds(0, BLK)], rows[:, pl.ds(BLK, BLK)])


def final(tab, pos, recv, front, rows, cols):
    def recv_spec(c):
        return pl.BlockSpec(
            (1, 8, 2, 1, BLK, BLK), lambda s, tab, pos: (jnp.maximum(tab[c, s], 0), 0, 0, c, 0, 0)
        )

    return pl.pallas_call(
        final_kernel,
        out_shape=jax.ShapeDtypeStruct((9 * BLK, 18 * BLK), F32),
        grid_spec=pltpu.PrefetchScalarGridSpec(
            num_scalar_prefetch=2,
            grid=(9,),
            in_specs=[
                recv_spec(0),
                recv_spec(1),
                pl.BlockSpec((BLK, 18 * BLK), lambda s, *_: (s, 0)),
                pl.BlockSpec((BLK, 2 * BLK), lambda s, *_: (s, 0)),
                pl.BlockSpec((18 * BLK, 2 * BLK), lambda s, *_: (0, 0)),
            ],
            out_specs=pl.BlockSpec((BLK, 18 * BLK), lambda s, *_: (s, 0)),
            scratch_shapes=[pltpu.VMEM((18 * BLK, 4 * BLK), BF16)],
        ),
        compiler_params=pltpu.CompilerParams(vmem_limit_bytes=40 << 20),
        name="final",
    )(tab, pos, recv, recv, front, rows, cols)


def shards(front_entries, children, child_maps):
    own_row = lax.axis_index("row")
    own_col = lax.axis_index("col")
    pos = jnp.stack([own_row, own_col]).astype(jnp.int32)
    packed = pack(children, child_maps, pos).reshape(32, 8, BLK, BLK)
    recv = lax.all_to_all(packed, ("row", "col"), split_axis=0, concat_axis=0, tiled=True)
    recv = recv.reshape(8, 8, 2, 2, BLK, BLK)
    tab = slot_tables(child_maps, own_row, own_col)
    mine = panel(recv, front_entries, tab)
    both = lax.psum(jnp.stack([jnp.where(own_col == p, mine, 0.0) for p in range(2)]), "col")
    rows = both.transpose(1, 0, 2).reshape(9 * BLK, 2 * BLK)
    every = lax.all_gather(rows.reshape(9, BLK, 2 * BLK), "row", axis=0)
    corner = every[:2, 0].reshape(2 * BLK, 2 * BLK)
    low = jnp.tril(jnp.linalg.cholesky(corner))
    inv = lax.linalg.triangular_solve(low, jnp.eye(2 * BLK, dtype=F32), left_side=True, lower=True)
    picked = jnp.stack([lax.dynamic_index_in_dim(every, own_col + 4 * h, 0, False) for h in range(2)], axis=1)
    cols = picked.reshape(18 * BLK, 2 * BLK)
    dims = (((1,), (1,)), ((), ()))
    rows = lax.dot_general(rows, inv, dims, precision=HIGH, preferred_element_type=F32)
    cols = lax.dot_general(cols, inv, dims, precision=HIGH, preferred_element_type=F32)
    return final(tab, pos, recv, front_entries, rows, cols)


def solution(mesh):
    in_specs = (P(("front", "row"), "col"), P("front", "row", "col"), P("front", None))
    out_specs = P(("front", "row"), "col")
    return jax.shard_map(shards, mesh=mesh, in_specs=in_specs, out_specs=out_specs, check_vma=False)
```

```python
import jax
import jax.numpy as jnp
from jax import lax
from jax.experimental import pallas as pl
from jax.experimental.pallas import tpu as pltpu
from jax.sharding import PartitionSpec as P

BLK = 128
F32 = jnp.float32
BF16 = jnp.bfloat16
HIGH = lax.Precision.HIGHEST


def pack_kernel(maps, pos, children, out, buf, packed, row_of, col_of, in_sem, out_sem):
    own_row, own_col = pos[0], pos[1]
    for c in range(2):
        for k in range(8):
            row_of[c, maps[c, k * 8 + own_row] % 8] = k
        for k in range(16):
            col_of[c, (k % 2) * 8 + maps[c, k * 4 + own_col] % 8] = k
    for d in range(8):
        for c in range(2):
            pltpu.make_async_copy(
                children.at[c, pl.ds(row_of[c, d] * BLK, BLK), :], buf.at[d, c], in_sem.at[d]
            ).start()

    def one_row(d, carry):
        for c in range(2):
            pltpu.make_async_copy(children.at[0, pl.ds(0, BLK), :], buf.at[d, c], in_sem.at[d]).wait()
        for c in range(2):
            for half in range(2):
                for delta in range(8):
                    start = pl.multiple_of(col_of[c, half * 8 + delta] * BLK, BLK)
                    packed[half, d % 4, delta % 4, d // 4, delta // 4, c] = buf[d, c, :, pl.ds(start, BLK)]
        pltpu.make_async_copy(
            packed.at[:, d % 4, :, d // 4], out.at[:, d % 4, :, d // 4], out_sem.at[0]
        ).start()
        return carry

    lax.fori_loop(0, 8, one_row, 0)
    pltpu.make_async_copy(packed, out, out_sem.at[0]).wait()


def pack(children, child_maps, pos):
    return pl.pallas_call(
        pack_kernel,
        out_shape=jax.ShapeDtypeStruct((2, 4, 4, 2, 2, 2, BLK, BLK), BF16),
        in_specs=[
            pl.BlockSpec(memory_space=pltpu.SMEM),
            pl.BlockSpec(memory_space=pltpu.SMEM),
            pl.BlockSpec(memory_space=pl.ANY),
        ],
        out_specs=pl.BlockSpec(memory_space=pl.ANY),
        scratch_shapes=[
            pltpu.VMEM((8, 2, BLK, 16 * BLK), BF16),
            pltpu.VMEM((2, 4, 4, 2, 2, 2, BLK, BLK), BF16),
            pltpu.SMEM((2, 8), jnp.int32),
            pltpu.SMEM((2, 16), jnp.int32),
            pltpu.SemaphoreType.DMA((8,)),
            pltpu.SemaphoreType.DMA((1,)),
        ],
        compiler_params=pltpu.CompilerParams(vmem_limit_bytes=40 << 20),
        name="pack",
    )(child_maps, pos, children)


def identity():
    r = lax.broadcasted_iota(jnp.int32, (BLK, BLK), 0)
    k = lax.broadcasted_iota(jnp.int32, (BLK, BLK), 1)
    return jnp.where(r == k, 1.0, 0.0).astype(BF16)


def place(row, col):
    return col // 2 * 2 + row % 2, row // 2, col % 2


def device(x, z, core):
    return {"row": z * 2 + x % 2, "col": x // 2 * 2 + core}


def ring(t):
    t = (t + 4) % 4
    return t - 2 * (t // 3)


def apart(x, z, tx, tz):
    return ring(tx - x) + ring(tz - z)


def wants(x, z, core, tx, tz, half):
    a, b = z * 2 + x % 2, x // 2 * 2 + core
    alpha = b + 4 * half
    ox, oz, _ = place(alpha, a % 4)
    here, there = apart(x, z, tx, tz), apart(ox, oz, tx, tz)
    return here <= there, here < there


def unit(packed, x, z, core, tx, tz, tcore, half, kind):
    a, b = z * 2 + x % 2, x // 2 * 2 + core
    alpha = b + 4 * half
    d, e = tz * 2 + tx % 2, tx // 2 * 2 + tcore
    if kind == 0:
        return packed.at[half, d % 4, e, d // 4], a * 8 + b * 2 + half
    return packed.at[half, e, d % 4, :, d // 4], alpha * 8 + a % 4 * 2 + a // 4


def far_step(n):
    k = n % 3
    return 2 - k + 3 * (k // 2), 1 + n // 6, n // 3 % 2


def near_step(n):
    dx = (1 - n // 6) * (1 - n // 12) * (n // 2 + 1)
    dz = n // 6 * (1 - n // 12) * ((n - 6) // 2 + 1)
    return dx, dz, n % 2 * (1 - n // 12) + n // 12


def greet_neighbours(barrier, x, z, core):
    def greet(n, carry):
        dx, dz, dc = near_step(n)
        pl.semaphore_signal(
            barrier, inc=1, device_id=device((x + dx) % 4, (z + dz) % 4, (core + dc) % 2),
            device_id_type=pl.DeviceIdType.MESH,
        )
        return carry

    lax.fori_loop(0, 13, greet, 0)
    pl.semaphore_wait(barrier, 13)


def exchange_kernel(packed, recv, hold, send_sem, recv_sem, hold_sem):
    x, z, core = place(lax.axis_index("row"), lax.axis_index("col"))
    barrier = pltpu.get_barrier_semaphore()

    greet_neighbours(barrier, x, z, core)

    def remote(src, dst, arrived, tx, tz, tcore):
        return pltpu.make_async_remote_copy(
            src_ref=src, dst_ref=dst, send_sem=send_sem, recv_sem=arrived,
            device_id=device(tx, tz, tcore), device_id_type=pl.DeviceIdType.MESH,
        )

    def far(n, act):
        dz, dx, dc = far_step(n)
        tx, tz, tcore = (x + dx) % 4, (z + dz) % 4, (core + dc) % 2
        for half in range(2):
            for kind, wanted in enumerate(wants(x, z, core, tx, tz, half)):
                src, _ = unit(packed, x, z, core, tx, tz, tcore, half, kind)
                slot = n * 4 + half * 2 + kind

                @pl.when(wanted)
                def _():
                    act(remote(src, hold.at[slot], hold_sem.at[slot], x, tz, core))

    def near(n, act):
        dx, dz, dc = near_step(n)
        tx, tz, tcore = (x + dx) % 4, (z + dz) % 4, (core + dc) % 2
        for half in range(2):
            for kind, wanted in enumerate(wants(x, z, core, tx, tz, half)):
                src, dst = unit(packed, x, z, core, tx, tz, tcore, half, kind)

                @pl.when(wanted)
                def _():
                    act(remote(src, recv.at[dst], recv_sem.at[dst], tx, tz, tcore))

    def start(n, carry):
        far(n, lambda copy: copy.start())

        @pl.when(n < 13)
        def _():
            near(n, lambda copy: copy.start())

        return carry

    lax.fori_loop(0, 18, start, 0)
    own = [wants(x, z, core, x, z, half) for half in range(2)]
    for half in range(2):
        for kind in range(2):
            src, dst = unit(packed, x, z, core, x, z, core, half, kind)

            @pl.when(own[half][kind])
            def _():
                pltpu.make_async_copy(src, recv.at[dst], recv_sem.at[dst]).start()

    def pass_on(n, act):
        dz, dx, dc = far_step(n)
        sz = (z - dz + 4) % 4
        tx, tcore = (x + dx) % 4, (core + dc) % 2
        for half in range(2):
            for kind, wanted in enumerate(wants(x, sz, core, tx, z, half)):
                _, dst = unit(packed, x, sz, core, tx, z, tcore, half, kind)
                slot = n * 4 + half * 2 + kind

                @pl.when(wanted)
                def _():
                    act(slot, remote(hold.at[slot], recv.at[dst], recv_sem.at[dst], tx, z, tcore))

    def forward(slot, copy):
        pltpu.make_async_copy(hold.at[slot], hold.at[slot], hold_sem.at[slot]).wait()
        copy.start()

    def relay(n, carry):
        pass_on(n, forward)
        return carry

    lax.fori_loop(0, 18, relay, 0)

    def finish(n, carry):
        far(n, lambda copy: copy.wait_send())
        pass_on(n, lambda slot, copy: copy.wait_send())

        @pl.when(n < 13)
        def _():
            near(n, lambda copy: copy.wait_send())

        return carry

    def settle(slot, carry):
        pltpu.make_async_copy(recv.at[slot], recv.at[slot], recv_sem.at[slot]).wait()
        row, u = slot // 8, slot % 8
        alpha = u // 2 + u % 2 * 4
        nx, nz, _ = place(row, alpha % 4)
        ox, oz, _ = place(alpha, row % 4)

        @pl.when(apart(ox, oz, x, z) < apart(nx, nz, x, z))
        def _():
            for h in range(2):
                for c in range(2):
                    recv[slot, h, c] = lax.dot_general(
                        identity(), recv[slot, h, c], (((1,), (1,)), ((), ())), preferred_element_type=F32
                    ).astype(BF16)

        return carry

    lax.fori_loop(0, 64, settle, 0)
    lax.fori_loop(0, 18, finish, 0)


def exchange(packed):
    return pl.pallas_call(
        exchange_kernel,
        out_shape=jax.ShapeDtypeStruct((64, 2, 2, BLK, BLK), BF16),
        in_specs=[pl.BlockSpec(memory_space=pl.ANY)],
        out_specs=pl.BlockSpec(memory_space=pltpu.VMEM),
        scratch_shapes=[
            pltpu.VMEM((72, 2, 2, BLK, BLK), BF16),
            pltpu.SemaphoreType.DMA(()),
            pltpu.SemaphoreType.DMA((64,)),
            pltpu.SemaphoreType.DMA((72,)),
        ],
        compiler_params=pltpu.CompilerParams(
            collective_id=0, has_side_effects=True, vmem_limit_bytes=40 << 20
        ),
        name="exchange",
    )(packed)


def slot_tables(child_maps, own_row, own_col):
    ids = jnp.arange(64, dtype=jnp.int32)
    rows = jnp.arange(9, dtype=jnp.int32) * 8 + own_row
    cols = jnp.arange(18, dtype=jnp.int32) * 4 + own_col
    unit = ids % 4 * 2 + ids % 8 // 4
    row_tab = jnp.max(jnp.where(child_maps[:, None, :] == rows[None, :, None], ids % 8, -1), axis=2)
    col_tab = jnp.max(jnp.where(child_maps[:, None, :] == cols[None, :, None], unit, -1), axis=2)
    a, u = row_tab[:, :, None], col_tab[:, None, :]
    code = jnp.where((a >= 0) & (u >= 0), u, -1)
    return jnp.maximum(row_tab, 0).astype(jnp.int32), code.astype(jnp.int32)


def panel_kernel(tab, code, recv, front, out, acc, sem):
    for s in range(9):
        out[s] = front[pl.ds(s * BLK, BLK), :].astype(F32)
    for c in range(2):
        for s in range(9):
            copy = pltpu.make_async_copy(
                recv.at[tab[c, s] * 8 + jnp.maximum(code[c, s, 0], 0) % 8, 0, c], acc.at[c * 9 + s], sem.at[c * 9 + s]
            )
            copy.start()
    for c in range(2):
        for s in range(9):
            pltpu.make_async_copy(recv.at[0, 0, 0], acc.at[c * 9 + s], sem.at[c * 9 + s]).wait()
            out[s] += jnp.where(code[c, s, 0] >= 0, acc[c * 9 + s].astype(F32), 0.0)


def panel(recv, front, tab, code):
    return pl.pallas_call(
        panel_kernel,
        out_shape=jax.ShapeDtypeStruct((9, BLK, BLK), F32),
        grid=(1,),
        in_specs=[
            pl.BlockSpec(memory_space=pltpu.SMEM),
            pl.BlockSpec(memory_space=pltpu.SMEM),
            pl.BlockSpec(memory_space=pl.ANY),
            pl.BlockSpec((9 * BLK, BLK), lambda i: (0, 0)),
        ],
        out_specs=pl.BlockSpec((9, BLK, BLK), lambda i: (0, 0, 0)),
        scratch_shapes=[pltpu.VMEM((18, BLK, BLK), BF16), pltpu.SemaphoreType.DMA((18,))],
        name="panel",
    )(tab, code, recv, front)


def split(x):
    hi = x.astype(BF16)
    lo = (x - hi.astype(F32)).astype(BF16)
    return hi, lo


def factor_rows(r, mat):
    lane = lax.broadcasted_iota(jnp.int32, (8, 2 * BLK), 1)
    wide = lax.broadcasted_iota(jnp.int32, (8, 4 * BLK), 1)
    sub = lax.broadcasted_iota(jnp.int32, (8, 1), 0)
    rows = pl.ds(pl.multiple_of(r * 8, 8), 8)
    w = mat[rows, :]
    head = w[:, : 2 * BLK]
    col = [jnp.sum(jnp.where(lane == r * 8 + j, head, 0.0), axis=1, keepdims=True) for j in range(8)]
    for j in range(8):
        pivot = col[j][j : j + 1]
        inv = lax.rsqrt(pivot)
        inv = inv * (1.5 - 0.5 * pivot * inv * inv)
        mult = jnp.where(sub > j, col[j] * inv, 0.0)
        for k in range(j + 1, 8):
            col[k] = col[k] - mult * (col[k][j : j + 1] * inv)
        top = w[j : j + 1] * inv
        w = jnp.where(sub == j, top, w - mult * top)
    w = jnp.where(wide < r * 8 + sub, 0.0, w)
    mat[rows, :] = w
    u = w[:, : 2 * BLK]
    update = lax.dot_general(u, w, (((0,), (0,)), ((), ())), precision=HIGH, preferred_element_type=F32)
    below = lax.broadcasted_iota(jnp.int32, (2 * BLK, 1), 0) >= (r + 1) * 8
    mat[...] = mat[...] - jnp.where(below, update, 0.0)


def spread_kernel(
    mine, rows_out, cols_out, rows, cols, column, corner, mat,
    send_sem, row_sem, column_sem, col_sem, corner_sem,
):
    x, z, core = place(lax.axis_index("row"), lax.axis_index("col"))
    owner = x < 2
    root = x // 2 == z % 2
    other = 1 - core
    side = x + 1 - x % 2 * 2

    def remote(src, dst, arrived, tx, tz, tcore):
        return pltpu.make_async_remote_copy(
            src_ref=src, dst_ref=dst, send_sem=send_sem, recv_sem=arrived,
            device_id=device(tx, tz, tcore), device_id_type=pl.DeviceIdType.MESH,
        )

    def arrive(ref, sem):
        pltpu.make_async_copy(ref, ref, sem).wait()

    def corner_out(act):
        @pl.when(owner & (z == 0))
        def _():
            for dz in range(1, 4):
                act(remote(mine.at[0], corner.at[x, core], corner_sem.at[x, core], x, (z + dz) % 4, core))

    def corner_across(act):
        @pl.when(owner)
        def _():
            for dx in range(1, 4):
                act(
                    remote(
                        corner.at[x, core], corner.at[x, core], corner_sem.at[x, core], (x + dx) % 4, z, core
                    )
                )

    def corner_swap(v, act):
        act(remote(corner.at[v, core], corner.at[v, core], corner_sem.at[v, core], x, z, other))

    def row_out(s, act):
        @pl.when(owner)
        def _():
            act(remote(mine.at[s], rows.at[core, s], row_sem.at[core, s], (x + 2) % 4, z, core))

    def row_swap(s, act):
        act(remote(rows.at[core, s], rows.at[core, s], row_sem.at[core, s], x, z, other))

    def down_column(s, act):
        @pl.when(root)
        def _():
            for dz in range(1, 4):
                act(
                    remote(
                        rows.at[core, s], column.at[z // 2, s], column_sem.at[z // 2, s], x, (z + dz) % 4, core
                    )
                )

    def to_side(n, act):
        h, s = n % 2, n // 2
        act(remote(column.at[h, s], cols.at[h, core, s], col_sem.at[h, core, s], side, z, x % 2))

        @pl.when(core != x % 2)
        def _():
            act(remote(column.at[h, s], cols.at[h, core, s], col_sem.at[h, core, s], x, z, other))

    start = lambda copy: copy.start()
    barrier = pltpu.get_barrier_semaphore()
    greet_neighbours(barrier, x, z, core)
    corner_out(start)

    @pl.when(owner & (z == 0))
    def _():
        pltpu.make_async_copy(mine.at[0], corner.at[x, core], corner_sem.at[x, core]).start()

    def first(s, carry):
        row_out(s, start)

        @pl.when(owner)
        def _():
            pltpu.make_async_copy(mine.at[s], rows.at[core, s], row_sem.at[core, s]).start()

        return carry

    lax.fori_loop(0, 9, first, 0)

    @pl.when(owner)
    def _():
        arrive(corner.at[x, core], corner_sem.at[x, core])

    corner_across(start)

    @pl.when(x != 0)
    def _():
        arrive(corner.at[0, core], corner_sem.at[0, core])

    corner_swap(0, start)

    @pl.when(x != 1)
    def _():
        arrive(corner.at[1, core], corner_sem.at[1, core])

    corner_swap(1, start)

    def second(s, carry):
        arrive(rows.at[core, s], row_sem.at[core, s])
        row_swap(s, start)
        down_column(s, start)

        @pl.when(root)
        def _():
            pltpu.make_async_copy(rows.at[core, s], column.at[z // 2, s], column_sem.at[z // 2, s]).start()

        return carry

    lax.fori_loop(0, 9, second, 0)
    for v in range(2):
        arrive(corner.at[v, other], corner_sem.at[v, other])
    r = lax.broadcasted_iota(jnp.int32, (2 * BLK, 2 * BLK), 0)
    k = lax.broadcasted_iota(jnp.int32, (2 * BLK, 2 * BLK), 1)
    mat[:, pl.ds(2 * BLK, 2 * BLK)] = jnp.where(r == k, 1.0, 0.0)
    for v in range(2):
        for p in range(2):
            mat[pl.ds(v * BLK, BLK), pl.ds(p * BLK, BLK)] = corner[v, p]

    def third(n, carry):
        h, s = n % 2, n // 2
        arrive(column.at[h, s], column_sem.at[h, s])
        to_side(n, start)

        @pl.when(core == x % 2)
        def _():
            pltpu.make_async_copy(column.at[h, s], cols.at[h, core, s], col_sem.at[h, core, s]).start()

        for part in range(2):

            @pl.when(n < 16)
            def _():
                factor_rows(n * 2 + part, mat)

        return carry

    lax.fori_loop(0, 18, third, 0)

    def solve(pair):
        return lax.dot_general(
            pair, mat[:, pl.ds(2 * BLK, 2 * BLK)], (((1,), (1,)), ((), ())),
            precision=HIGH, preferred_element_type=F32,
        )

    def solve_row(s, carry):
        arrive(rows.at[other, s], row_sem.at[other, s])
        rows_out[s] = solve(jnp.concatenate([rows[0, s], rows[1, s]], axis=1))
        return carry

    lax.fori_loop(0, 9, solve_row, 0)

    def solve_col(n, carry):
        h, s = n % 2, n // 2
        for p in range(2):
            arrive(cols.at[h, p, s], col_sem.at[h, p, s])
        hi, lo = split(solve(jnp.concatenate([cols[h, 0, s], cols[h, 1, s]], axis=1)))
        cols_out[n, :, pl.ds(0, 2 * BLK)] = hi
        cols_out[n, :, pl.ds(2 * BLK, 2 * BLK)] = lo
        return carry

    lax.fori_loop(0, 18, solve_col, 0)
    done = lambda copy: copy.wait_send()
    corner_out(done)
    corner_across(done)
    for v in range(2):
        corner_swap(v, done)

    def last(s, carry):
        row_out(s, done)
        row_swap(s, done)
        down_column(s, done)
        to_side(s * 2, done)
        to_side(s * 2 + 1, done)
        return carry

    lax.fori_loop(0, 9, last, 0)


def spread(mine):
    return pl.pallas_call(
        spread_kernel,
        out_shape=(
            jax.ShapeDtypeStruct((9, BLK, 2 * BLK), F32),
            jax.ShapeDtypeStruct((18, BLK, 4 * BLK), BF16),
        ),
        in_specs=[pl.BlockSpec(memory_space=pltpu.VMEM)],
        out_specs=(pl.BlockSpec(memory_space=pltpu.VMEM), pl.BlockSpec(memory_space=pltpu.VMEM)),
        scratch_shapes=[
            pltpu.VMEM((2, 9, BLK, BLK), F32),
            pltpu.VMEM((2, 2, 9, BLK, BLK), F32),
            pltpu.VMEM((2, 9, BLK, BLK), F32),
            pltpu.VMEM((2, 2, BLK, BLK), F32),
            pltpu.VMEM((2 * BLK, 4 * BLK), F32),
            pltpu.SemaphoreType.DMA(()),
            pltpu.SemaphoreType.DMA((2, 9)),
            pltpu.SemaphoreType.DMA((2, 9)),
            pltpu.SemaphoreType.DMA((2, 2, 9)),
            pltpu.SemaphoreType.DMA((2, 2)),
        ],
        compiler_params=pltpu.CompilerParams(
            collective_id=1, has_side_effects=True, vmem_limit_bytes=40 << 20
        ),
        name="spread",
    )(mine)


def final_kernel(tab, code, pos, recv0, recv1, front, rows, cols, out):
    s = pl.program_id(0)
    own_row, own_col = pos[0], pos[1]

    lead = (s == 0) & (own_row < 2)

    @pl.when(lead)
    def _():
        out[...] = jnp.zeros_like(out)

        @pl.when(own_col < 2)
        def _():
            r = lax.broadcasted_iota(jnp.int32, (BLK, BLK), 0) + own_row * BLK
            k = lax.broadcasted_iota(jnp.int32, (BLK, BLK), 1) + own_col * BLK
            mine = jnp.where(own_col == 0, rows[0, :, pl.ds(0, BLK)], rows[0, :, pl.ds(BLK, BLK)])
            out[:, pl.ds(0, BLK)] = jnp.where(r >= k, mine, 0.0)

    @pl.when(jnp.logical_not(lead))
    def _():
        hi, lo = split(rows[0])
        left = jnp.concatenate([hi, lo, hi], axis=1)
        for t in range(18):
            part = pl.ds(t * BLK, BLK)
            right = jnp.concatenate(
                [cols[t, :, pl.ds(0, 256)], cols[t, :, pl.ds(0, 256)], cols[t, :, pl.ds(256, 256)]], axis=1
            )
            val = front[:, part].astype(F32) - lax.dot_general(
                left, right, (((1,), (1,)), ((), ())), preferred_element_type=F32
            )
            for c, recv in enumerate((recv0, recv1)):
                u = code[c, s, t]
                val += jnp.where(u >= 0, recv[0, jnp.maximum(u, 0), t % 2, 0].astype(F32), 0.0)
            out[:, part] = val

        @pl.when(own_col < 2)
        def _():
            out[:, pl.ds(0, BLK)] = jnp.where(own_col == 0, rows[0, :, pl.ds(0, BLK)], rows[0, :, pl.ds(BLK, BLK)])


def final(tab, code, pos, recv, front, rows, cols):
    def recv_spec(c):
        return pl.BlockSpec(
            (1, 8, 2, 1, BLK, BLK), lambda s, tab, code, pos: (tab[c, s], 0, 0, c, 0, 0)
        )

    return pl.pallas_call(
        final_kernel,
        out_shape=jax.ShapeDtypeStruct((9 * BLK, 18 * BLK), F32),
        grid_spec=pltpu.PrefetchScalarGridSpec(
            num_scalar_prefetch=3,
            grid=(9,),
            in_specs=[
                recv_spec(0),
                recv_spec(1),
                pl.BlockSpec((BLK, 18 * BLK), lambda s, *_: (s, 0)),
                pl.BlockSpec((1, BLK, 2 * BLK), lambda s, *_: (s, 0, 0)),
                pl.BlockSpec((18, BLK, 4 * BLK), lambda s, *_: (0, 0, 0)),
            ],
            out_specs=pl.BlockSpec((BLK, 18 * BLK), lambda s, *_: (s, 0)),
        ),
        compiler_params=pltpu.CompilerParams(vmem_limit_bytes=40 << 20),
        name="final",
    )(tab, code, pos, recv, recv, front, rows, cols)


def shards(front_entries, children, child_maps):
    own_row = lax.axis_index("row")
    own_col = lax.axis_index("col")
    pos = jnp.stack([own_row, own_col]).astype(jnp.int32)
    recv = exchange(pack(children, child_maps, pos))
    tab, code = slot_tables(child_maps, own_row, own_col)
    mine = panel(recv, front_entries, tab, code)
    recv = recv.reshape(8, 8, 2, 2, BLK, BLK)
    rows, cols = spread(mine)
    return final(tab, code, pos, recv, front_entries, rows, cols)


def solution(mesh):
    in_specs = (P(("front", "row"), "col"), P("front", "row", "col"), P("front", None))
    out_specs = P(("front", "row"), "col")
    return jax.shard_map(shards, mesh=mesh, in_specs=in_specs, out_specs=out_specs, check_vma=False)
```

```python
import jax
import jax.numpy as jnp
from jax import lax
from jax.experimental import pallas as pl
from jax.experimental.pallas import tpu as pltpu
from jax.sharding import PartitionSpec as P

BLK = 128
F32 = jnp.float32
BF16 = jnp.bfloat16
HIGH = lax.Precision.HIGHEST


def pack_kernel(maps, children, out, rows_of, cols_of, buf, packed, row_of, col_of, in_sem, out_sem):
    own_row, own_col = lax.axis_index("row"), lax.axis_index("col")
    for c in range(2):
        for k in range(8):
            row_of[c, maps[c, k * 8 + own_row] % 8] = k
        for k in range(16):
            col_of[c, (k % 2) * 8 + maps[c, k * 4 + own_col] % 8] = k
    for d in range(8):
        for c in range(2):
            pltpu.make_async_copy(
                children.at[c, pl.ds(row_of[c, d] * BLK, BLK), :], buf.at[d, c], in_sem.at[d]
            ).start()
    for c in range(2):
        for s in range(9):
            rows_of[c, s] = -1
        for t in range(18):
            cols_of[c, t] = -1

        def look(k, carry):
            v = maps[c, k]

            @pl.when(v % 8 == own_row)
            def _():
                rows_of[c, v // 8] = k % 8

            @pl.when(v % 4 == own_col)
            def _():
                cols_of[c, v // 4] = k % 4 * 2 + k % 8 // 4

            return carry

        lax.fori_loop(0, 64, look, 0, unroll=8)

    def one_row(d, carry):
        for c in range(2):
            pltpu.make_async_copy(children.at[0, pl.ds(0, BLK), :], buf.at[d, c], in_sem.at[d]).wait()
        for c in range(2):
            for half in range(2):
                for delta in range(8):
                    start = pl.multiple_of(col_of[c, half * 8 + delta] * BLK, BLK)
                    packed[half, d % 4, delta % 4, d // 4, delta // 4, c] = buf[d, c, :, pl.ds(start, BLK)]
        pltpu.make_async_copy(
            packed.at[:, d % 4, :, d // 4], out.at[:, d % 4, :, d // 4], out_sem.at[0]
        ).start()
        return carry

    lax.fori_loop(0, 8, one_row, 0)
    pltpu.make_async_copy(packed, out, out_sem.at[0]).wait()


def pack(children, child_maps):
    return pl.pallas_call(
        pack_kernel,
        out_shape=(
            jax.ShapeDtypeStruct((2, 4, 4, 2, 2, 2, BLK, BLK), BF16),
            jax.ShapeDtypeStruct((2, 9), jnp.int32),
            jax.ShapeDtypeStruct((2, 18), jnp.int32),
        ),
        in_specs=[pl.BlockSpec(memory_space=pltpu.SMEM), pl.BlockSpec(memory_space=pl.ANY)],
        out_specs=(
            pl.BlockSpec(memory_space=pl.ANY),
            pl.BlockSpec(memory_space=pltpu.SMEM),
            pl.BlockSpec(memory_space=pltpu.SMEM),
        ),
        scratch_shapes=[
            pltpu.VMEM((8, 2, BLK, 16 * BLK), BF16),
            pltpu.VMEM((2, 4, 4, 2, 2, 2, BLK, BLK), BF16),
            pltpu.SMEM((2, 8), jnp.int32),
            pltpu.SMEM((2, 16), jnp.int32),
            pltpu.SemaphoreType.DMA((8,)),
            pltpu.SemaphoreType.DMA((1,)),
        ],
        compiler_params=pltpu.CompilerParams(vmem_limit_bytes=60 << 20),
        name="pack",
    )(child_maps, children)


def identity():
    r = lax.broadcasted_iota(jnp.int32, (BLK, BLK), 0)
    k = lax.broadcasted_iota(jnp.int32, (BLK, BLK), 1)
    return jnp.where(r == k, 1.0, 0.0).astype(BF16)


def place(row, col):
    return col // 2 * 2 + row % 2, row // 2, col % 2


def device(x, z, core):
    return {"row": z * 2 + x % 2, "col": x // 2 * 2 + core}


def ring(t):
    t = (t + 4) % 4
    return t - 2 * (t // 3)


def apart(x, z, tx, tz):
    return ring(tx - x) + ring(tz - z)


def wants(x, z, core, tx, tz, half):
    a, b = z * 2 + x % 2, x // 2 * 2 + core
    alpha = b + 4 * half
    ox, oz, _ = place(alpha, a % 4)
    here, there = apart(x, z, tx, tz), apart(ox, oz, tx, tz)
    return here <= there, here < there


def unit(packed, x, z, core, tx, tz, tcore, half, kind, h):
    a, b = z * 2 + x % 2, x // 2 * 2 + core
    alpha = b + 4 * half
    d, e = tz * 2 + tx % 2, tx // 2 * 2 + tcore
    if kind == 0:
        return packed.at[half, d % 4, e, d // 4, h], a * 8 + b * 2 + half
    return packed.at[half, e, d % 4, h, d // 4], alpha * 8 + a % 4 * 2 + a // 4


def far_step(n):
    k = n % 3
    return 2 - k + 3 * (k // 2), 1 + n // 6, n // 3 % 2


def near_step(n):
    dx = (1 - n // 6) * (1 - n // 12) * (n // 2 + 1)
    dz = n // 6 * (1 - n // 12) * ((n - 6) // 2 + 1)
    return dx, dz, n % 2 * (1 - n // 12) + n // 12


def greet_neighbours(barrier, x, z, core):
    def greet(n, carry):
        dx, dz, dc = near_step(n)
        pl.semaphore_signal(
            barrier, inc=1, device_id=device((x + dx) % 4, (z + dz) % 4, (core + dc) % 2),
            device_id_type=pl.DeviceIdType.MESH,
        )
        return carry

    lax.fori_loop(0, 13, greet, 0)
    pl.semaphore_wait(barrier, 13)


def split(x):
    hi = x.astype(BF16)
    lo = (x - hi.astype(F32)).astype(BF16)
    return hi, lo


def pieces(x):
    a = x.astype(BF16).astype(F32)
    b = (x - a).astype(BF16).astype(F32)
    return a, b, x - a - b


def factor_rows(r, mat, base):
    span = pl.ds(base, 3 * BLK)
    lane = lax.broadcasted_iota(jnp.int32, (8, 2 * BLK - base), 1) + base
    wide = lax.broadcasted_iota(jnp.int32, (8, 3 * BLK), 1) + base
    sub = lax.broadcasted_iota(jnp.int32, (8, 1), 0)
    rows = pl.ds(pl.multiple_of(r * 8, 8), 8)
    w = mat[rows, span]
    head = w[:, : 2 * BLK - base]
    col = [jnp.sum(jnp.where(lane == r * 8 + j, head, 0.0), axis=1, keepdims=True) for j in range(8)]
    for j in range(8):
        pivot = col[j][j : j + 1]
        inv = lax.rsqrt(pivot)
        inv = inv * (1.5 - 0.5 * pivot * inv * inv)
        mult = jnp.where(sub > j, col[j] * inv, 0.0)
        for k in range(j + 1, 8):
            col[k] = col[k] - mult * (col[k][j : j + 1] * inv)
        top = w[j : j + 1] * inv
        w = jnp.where(sub == j, top, w - mult * top)
    w = jnp.where(wide < r * 8 + sub, 0.0, w)
    mat[rows, span] = w
    a, b, c = pieces(w)
    u = [part[:, : 2 * BLK - base] for part in (a, a, b, a, c, b)]
    left = jnp.concatenate(u, axis=0).astype(BF16)
    right = jnp.concatenate([a, b, a, c, a, b], axis=0).astype(BF16)
    update = lax.dot_general(left, right, (((0,), (0,)), ((), ())), preferred_element_type=F32)
    below = lax.broadcasted_iota(jnp.int32, (2 * BLK - base, 1), 0) + base >= (r + 1) * 8
    rest = pl.ds(base, 2 * BLK - base)
    mat[rest, span] = mat[rest, span] - jnp.where(below, update, 0.0)


def front_kernel(
    row_tab, col_tab, packed, front, out_a, out_b, rows_out, cols_out,
    recv_a, recv_b, hold, mine, rows, cols, column, corner, mat, rows_sol, cols_sol, inv,
    send_sem, recv_sem, hold_sem, row_sem, column_sem, col_sem, corner_sem, out_sem,
):
    x, z, core = place(lax.axis_index("row"), lax.axis_index("col"))
    owner = x < 2
    root = x // 2 == z % 2
    other = 1 - core
    side = x + 1 - x % 2 * 2
    recv = (recv_a, recv_b)
    start = lambda copy: copy.start()
    done = lambda copy: copy.wait_send()

    def remote(src, dst, arrived, tx, tz, tcore):
        return pltpu.make_async_remote_copy(
            src_ref=src, dst_ref=dst, send_sem=send_sem, recv_sem=arrived,
            device_id=device(tx, tz, tcore), device_id_type=pl.DeviceIdType.MESH,
        )

    def arrive(ref, sem):
        pltpu.make_async_copy(ref, ref, sem).wait()

    def loop(lo, hi, body):
        def step(n, carry):
            body(n)
            return carry

        lax.fori_loop(lo, hi, step, 0)

    def each(sx, sz, tx, tz, fn):
        for half in range(2):
            for kind, wanted in enumerate(wants(sx, sz, core, tx, tz, half)):
                for h in range(2):

                    @pl.when(wanted)
                    def _():
                        fn(half, kind, h)

    def far(n, act):
        dz, dx, dc = far_step(n)
        tx, tz, tcore = (x + dx) % 4, (z + dz) % 4, (core + dc) % 2

        def one(half, kind, h):
            src, _ = unit(packed, x, z, core, tx, tz, tcore, half, kind, h)
            slot = n * 4 + half * 2 + kind
            act(remote(src, hold.at[slot, h], hold_sem.at[slot, h], x, tz, core))

        each(x, z, tx, tz, one)

    def near(n, act):
        dx, dz, dc = near_step(n)
        tx, tz, tcore = (x + dx) % 4, (z + dz) % 4, (core + dc) % 2

        def one(half, kind, h):
            src, dst = unit(packed, x, z, core, tx, tz, tcore, half, kind, h)
            act(remote(src, recv[h].at[dst], recv_sem.at[dst, h], tx, tz, tcore))

        each(x, z, tx, tz, one)

    def own():
        def one(half, kind, h):
            src, dst = unit(packed, x, z, core, x, z, core, half, kind, h)
            pltpu.make_async_copy(src, recv[h].at[dst], recv_sem.at[dst, h]).start()

        each(x, z, x, z, one)

    def pass_on(n, act, wait):
        dz, dx, dc = far_step(n)
        sz = (z - dz + 4) % 4
        tx, tcore = (x + dx) % 4, (core + dc) % 2

        def one(half, kind, h):
            _, dst = unit(packed, x, sz, core, tx, z, tcore, half, kind, h)
            slot = n * 4 + half * 2 + kind
            if wait:
                arrive(hold.at[slot, h], hold_sem.at[slot, h])
            act(remote(hold.at[slot, h], recv[h].at[dst], recv_sem.at[dst, h], tx, z, tcore))

        each(x, sz, tx, z, one)

    def settle(slot, h):
        arrive(recv[h].at[slot], recv_sem.at[slot, h])
        row, u = slot // 8, slot % 8
        alpha = u // 2 + u % 2 * 4
        nx, nz, _ = place(row, alpha % 4)
        ox, oz, _ = place(alpha, row % 4)

        @pl.when(apart(ox, oz, x, z) < apart(nx, nz, x, z))
        def _():
            for c in range(2):
                recv[h][slot, c] = lax.dot_general(
                    identity(), recv[h][slot, c], (((1,), (1,)), ((), ())), preferred_element_type=F32
                ).astype(BF16)

    def corner_out(act):
        @pl.when(owner & (z == 0))
        def _():
            for dz in range(1, 4):
                act(remote(mine.at[0], corner.at[x, core], corner_sem.at[x, core], x, (z + dz) % 4, core))

    def corner_across(act):
        @pl.when(owner)
        def _():
            for dx in range(1, 4):
                act(
                    remote(
                        corner.at[x, core], corner.at[x, core], corner_sem.at[x, core], (x + dx) % 4, z, core
                    )
                )

    def corner_swap(v, act):
        act(remote(corner.at[v, core], corner.at[v, core], corner_sem.at[v, core], x, z, other))

    def row_out(s, act):
        @pl.when(owner)
        def _():
            act(remote(mine.at[s], rows.at[core, s], row_sem.at[core, s], (x + 2) % 4, z, core))

    def row_swap(s, act):
        act(remote(rows.at[core, s], rows.at[core, s], row_sem.at[core, s], x, z, other))

    def down_column(s, act):
        @pl.when(root)
        def _():
            for dz in range(1, 4):
                act(
                    remote(
                        rows.at[core, s], column.at[z // 2, s], column_sem.at[z // 2, s], x, (z + dz) % 4, core
                    )
                )

    def to_side(n, act):
        h, s = n % 2, n // 2
        act(remote(column.at[h, s], cols.at[h, core, s], col_sem.at[h, core, s], side, z, x % 2))

        @pl.when(core != x % 2)
        def _():
            act(remote(column.at[h, s], cols.at[h, core, s], col_sem.at[h, core, s], x, z, other))

    barrier = pltpu.get_barrier_semaphore()
    greet_neighbours(barrier, x, z, core)

    loop(0, 6, lambda n: near(n, start))
    loop(0, 18, lambda n: far(n, start))
    loop(6, 13, lambda n: near(n, start))
    own()
    loop(0, 18, lambda n: pass_on(n, start, True))
    @pl.when(owner)
    def _():
        loop(0, 64, lambda slot: settle(slot, 0))
        for s in range(9):
            total = front[pl.ds(s * BLK, BLK), :].astype(F32)
            for c in range(2):
                row, u = row_tab[c, s], col_tab[c, 0]
                blk = recv_a[jnp.maximum(row, 0) * 8 + jnp.maximum(u, 0), c].astype(F32)
                total += jnp.where((row >= 0) & (u >= 0), blk, 0.0)
            mine[s] = total

    corner_out(start)

    @pl.when(owner & (z == 0))
    def _():
        pltpu.make_async_copy(mine.at[0], corner.at[x, core], corner_sem.at[x, core]).start()

    def first(s):
        row_out(s, start)

        @pl.when(owner)
        def _():
            pltpu.make_async_copy(mine.at[s], rows.at[core, s], row_sem.at[core, s]).start()

    loop(0, 9, first)

    def second(s):
        arrive(rows.at[core, s], row_sem.at[core, s])
        row_swap(s, start)
        down_column(s, start)

        @pl.when(root)
        def _():
            pltpu.make_async_copy(rows.at[core, s], column.at[z // 2, s], column_sem.at[z // 2, s]).start()

    loop(0, 9, second)

    @pl.when(owner)
    def _():
        arrive(corner.at[x, core], corner_sem.at[x, core])

    corner_across(start)

    @pl.when(x != 0)
    def _():
        arrive(corner.at[0, core], corner_sem.at[0, core])

    corner_swap(0, start)

    @pl.when(x != 1)
    def _():
        arrive(corner.at[1, core], corner_sem.at[1, core])

    corner_swap(1, start)
    for v in range(2):
        arrive(corner.at[v, other], corner_sem.at[v, other])
    r = lax.broadcasted_iota(jnp.int32, (2 * BLK, 2 * BLK), 0)
    k = lax.broadcasted_iota(jnp.int32, (2 * BLK, 2 * BLK), 1)
    mat[:, pl.ds(2 * BLK, 2 * BLK)] = jnp.where(r == k, 1.0, 0.0)
    for v in range(2):
        for p in range(2):
            mat[pl.ds(v * BLK, BLK), pl.ds(p * BLK, BLK)] = corner[v, p]

    def fourth(n):
        h, s = n % 2, n // 2
        arrive(column.at[h, s], column_sem.at[h, s])
        to_side(n, start)

        @pl.when(core == x % 2)
        def _():
            pltpu.make_async_copy(column.at[h, s], cols.at[h, core, s], col_sem.at[h, core, s]).start()

        for g in range(2):

            @pl.when((n >= g * 8) & (n < g * 8 + 8))
            def _():
                factor_rows(n * 2, mat, g * BLK)
                factor_rows(n * 2 + 1, mat, g * BLK)

    loop(0, 18, fourth)

    inv_hi, inv_lo = split(mat[:, pl.ds(2 * BLK, 2 * BLK)])
    inv[:, pl.ds(0, 2 * BLK)] = inv_hi
    inv[:, pl.ds(2 * BLK, 2 * BLK)] = inv_hi
    inv[:, pl.ds(4 * BLK, 2 * BLK)] = inv_lo

    def solve(left, right):
        pair = jnp.concatenate([left.reshape(3 * BLK, BLK), right.reshape(3 * BLK, BLK)], axis=1)
        hi, lo = split(pair)
        return lax.dot_general(
            jnp.concatenate([hi, lo, hi], axis=1), inv[...], (((1,), (1,)), ((), ())), preferred_element_type=F32
        )

    def solve_row(i):
        for j in range(3):
            arrive(rows.at[other, i * 3 + j], row_sem.at[other, i * 3 + j])
        three = pl.ds(i * 3, 3)
        rows_sol[three] = solve(rows[0, three], rows[1, three]).reshape(3, BLK, 2 * BLK)

    loop(0, 3, solve_row)

    def late(slot):
        settle(slot, 1)

        @pl.when(jnp.logical_not(owner))
        def _():
            settle(slot, 0)

    loop(0, 64, late)
    outs = [
        pltpu.make_async_copy(recv_a, out_a, out_sem.at[0]),
        pltpu.make_async_copy(recv_b, out_b, out_sem.at[1]),
        pltpu.make_async_copy(rows_sol, rows_out, out_sem.at[2]),
    ]
    for copy in outs:
        copy.start()

    def solve_col(n):
        h, i = n % 2, n // 2
        for p in range(2):
            for j in range(3):
                arrive(cols.at[h, p, i * 3 + j], col_sem.at[h, p, i * 3 + j])
        three = pl.ds(i * 3, 3)
        hi, lo = split(solve(cols[h, 0, three], cols[h, 1, three]).reshape(3, BLK, 2 * BLK))
        cols_sol[h, three, :, pl.ds(0, 2 * BLK)] = hi
        cols_sol[h, three, :, pl.ds(2 * BLK, 2 * BLK)] = lo

    loop(0, 6, solve_col)
    last = pltpu.make_async_copy(cols_sol, cols_out, out_sem.at[3])
    last.start()

    def finish(n):
        far(n, done)
        pass_on(n, done, False)

        @pl.when(n < 13)
        def _():
            near(n, done)

        to_side(n, done)

        @pl.when(n < 9)
        def _():
            row_out(n, done)
            row_swap(n, done)
            down_column(n, done)

    loop(0, 18, finish)
    corner_out(done)
    corner_across(done)
    for v in range(2):
        corner_swap(v, done)
    for copy in outs:
        copy.wait()
    last.wait()


def front_stage(row_tab, col_tab, packed, front):
    anywhere = pl.BlockSpec(memory_space=pl.ANY)
    return pl.pallas_call(
        front_kernel,
        grid=(1,),
        out_shape=(
            jax.ShapeDtypeStruct((64, 2, BLK, BLK), BF16),
            jax.ShapeDtypeStruct((64, 2, BLK, BLK), BF16),
            jax.ShapeDtypeStruct((9, BLK, 2 * BLK), F32),
            jax.ShapeDtypeStruct((2, 9, BLK, 4 * BLK), BF16),
        ),
        in_specs=[
            pl.BlockSpec(memory_space=pltpu.SMEM),
            pl.BlockSpec(memory_space=pltpu.SMEM),
            anywhere,
            pl.BlockSpec((9 * BLK, BLK), lambda i: (0, 0)),
        ],
        out_specs=(anywhere, anywhere, anywhere, anywhere),
        scratch_shapes=[
            pltpu.VMEM((64, 2, BLK, BLK), BF16),
            pltpu.VMEM((64, 2, BLK, BLK), BF16),
            pltpu.VMEM((72, 2, 2, BLK, BLK), BF16),
            pltpu.VMEM((9, BLK, BLK), F32),
            pltpu.VMEM((2, 9, BLK, BLK), F32),
            pltpu.VMEM((2, 2, 9, BLK, BLK), F32),
            pltpu.VMEM((2, 9, BLK, BLK), F32),
            pltpu.VMEM((2, 2, BLK, BLK), F32),
            pltpu.VMEM((2 * BLK, 4 * BLK), F32),
            pltpu.VMEM((9, BLK, 2 * BLK), F32),
            pltpu.VMEM((2, 9, BLK, 4 * BLK), BF16),
            pltpu.VMEM((2 * BLK, 6 * BLK), BF16),
            pltpu.SemaphoreType.DMA(()),
            pltpu.SemaphoreType.DMA((64, 2)),
            pltpu.SemaphoreType.DMA((72, 2)),
            pltpu.SemaphoreType.DMA((2, 9)),
            pltpu.SemaphoreType.DMA((2, 9)),
            pltpu.SemaphoreType.DMA((2, 2, 9)),
            pltpu.SemaphoreType.DMA((2, 2)),
            pltpu.SemaphoreType.DMA((4,)),
        ],
        compiler_params=pltpu.CompilerParams(
            collective_id=0, has_side_effects=True, vmem_limit_bytes=62 << 20
        ),
        name="front_stage",
    )(row_tab, col_tab, packed, front)


def final_kernel(row_tab, col_tab, *refs):
    recv = [refs[4 * j : 4 * j + 4] for j in range(3)]
    front, rows, cols, out = refs[12:]
    step = pl.program_id(0)
    own_row, own_col = lax.axis_index("row"), lax.axis_index("col")
    hi, lo = split(rows[...].reshape(3 * BLK, 2 * BLK))
    left = jnp.concatenate([hi, lo, hi], axis=1)
    for t in range(18):
        part = pl.ds(t * BLK, BLK)
        right = jnp.concatenate([cols[t % 2, t // 2, :, pl.ds(k, 256)] for k in (0, 0, 256)], axis=1)
        val = front[:, part].astype(F32) - lax.dot_general(
            left, right, (((1,), (1,)), ((), ())), preferred_element_type=F32
        )
        for j in range(3):
            here = val[j * BLK : (j + 1) * BLK]
            for c in range(2):
                u = col_tab[c, t]
                blk = recv[j][c * 2 + t % 2][0, jnp.maximum(u, 0), 0].astype(F32)
                here += jnp.where((u >= 0) & (row_tab[c, step * 3 + j] >= 0), blk, 0.0)
            out[pl.ds(j * BLK, BLK), part] = here

    @pl.when(own_col < 2)
    def _():
        for j in range(3):
            out[pl.ds(j * BLK, BLK), pl.ds(0, BLK)] = jnp.where(
                own_col == 0, rows[j, :, pl.ds(0, BLK)], rows[j, :, pl.ds(BLK, BLK)]
            )

    @pl.when((step == 0) & (own_row < 2))
    def _():
        out[pl.ds(0, BLK), :] = jnp.zeros((BLK, 18 * BLK), F32)

        @pl.when(own_col < 2)
        def _():
            r = lax.broadcasted_iota(jnp.int32, (BLK, BLK), 0) + own_row * BLK
            k = lax.broadcasted_iota(jnp.int32, (BLK, BLK), 1) + own_col * BLK
            mine = jnp.where(own_col == 0, rows[0, :, pl.ds(0, BLK)], rows[0, :, pl.ds(BLK, BLK)])
            out[pl.ds(0, BLK), pl.ds(0, BLK)] = jnp.where(r >= k, mine, 0.0)


def final(row_tab, col_tab, recv_a, recv_b, front, rows, cols):
    def recv_spec(j, c):
        return pl.BlockSpec(
            (1, 8, 1, BLK, BLK),
            lambda step, row_tab, col_tab: (jnp.maximum(row_tab[c, step * 3 + j], 0), 0, c, 0, 0),
        )

    return pl.pallas_call(
        final_kernel,
        out_shape=jax.ShapeDtypeStruct((9 * BLK, 18 * BLK), F32),
        grid_spec=pltpu.PrefetchScalarGridSpec(
            num_scalar_prefetch=2,
            grid=(3,),
            in_specs=[recv_spec(j, c) for j in range(3) for c in range(2) for _ in range(2)]
            + [
                pl.BlockSpec((3 * BLK, 18 * BLK), lambda s, *_: (s, 0)),
                pl.BlockSpec((3, BLK, 2 * BLK), lambda s, *_: (s, 0, 0)),
                pl.BlockSpec((2, 9, BLK, 4 * BLK), lambda s, *_: (0, 0, 0, 0)),
            ],
            out_specs=pl.BlockSpec((3 * BLK, 18 * BLK), lambda s, *_: (s, 0)),
        ),
        compiler_params=pltpu.CompilerParams(vmem_limit_bytes=60 << 20),
        name="final",
    )(row_tab, col_tab, *([recv_a, recv_b] * 6), front, rows, cols)


def shards(front_entries, children, child_maps):
    packed, row_tab, col_tab = pack(children, child_maps)
    recv_a, recv_b, rows, cols = front_stage(row_tab, col_tab, packed, front_entries)
    recv_a, recv_b = (part.reshape(8, 8, 2, BLK, BLK) for part in (recv_a, recv_b))
    return final(row_tab, col_tab, recv_a, recv_b, front_entries, rows, cols)


def solution(mesh):
    in_specs = (P(("front", "row"), "col"), P("front", "row", "col"), P("front", None))
    out_specs = P(("front", "row"), "col")
    return jax.shard_map(shards, mesh=mesh, in_specs=in_specs, out_specs=out_specs, check_vma=False)
```

```python
import jax
import jax.numpy as jnp
from jax import lax
from jax.experimental import pallas as pl
from jax.experimental.pallas import tpu as pltpu
from jax.sharding import PartitionSpec as P

BLK = 128
F32 = jnp.float32
BF16 = jnp.bfloat16
HIGH = lax.Precision.HIGHEST


def pack_kernel(maps, children, out, rows_of, cols_of, buf, packed, row_of, col_of, in_sem, out_sem):
    own_row, own_col = lax.axis_index("row"), lax.axis_index("col")
    for c in range(2):
        for k in range(8):
            row_of[c, maps[c, k * 8 + own_row] & 7] = k
        for k in range(16):
            col_of[c, (k % 2) * 8 + (maps[c, k * 4 + own_col] & 7)] = k
    for d in range(8):
        for c in range(2):
            pltpu.make_async_copy(
                children.at[c, pl.ds(row_of[c, d] * BLK, BLK), :], buf.at[d, c], in_sem.at[d]
            ).start()
    for c in range(2):
        for s in range(9):
            rows_of[c, s] = -1
        for t in range(18):
            cols_of[c, t] = -1

        for k in range(64):
            v = maps[c, k]

            @pl.when((v & 7) == own_row)
            def _():
                rows_of[c, v >> 3] = k % 8

            @pl.when((v & 3) == own_col)
            def _():
                cols_of[c, v >> 2] = k % 4 * 2 + k % 8 // 4

    def one_row(d, carry):
        for c in range(2):
            pltpu.make_async_copy(children.at[0, pl.ds(0, BLK), :], buf.at[d, c], in_sem.at[d]).wait()
        for c in range(2):
            for half in range(2):
                for delta in range(8):
                    start = pl.multiple_of(col_of[c, half * 8 + delta] * BLK, BLK)
                    packed[half, d % 4, delta % 4, d // 4, delta // 4, c] = buf[d, c, :, pl.ds(start, BLK)]
        pltpu.make_async_copy(
            packed.at[:, d % 4, :, d // 4], out.at[:, d % 4, :, d // 4], out_sem.at[0]
        ).start()
        return carry

    lax.fori_loop(0, 8, one_row, 0)
    pltpu.make_async_copy(packed, out, out_sem.at[0]).wait()


def pack(children, child_maps):
    return pl.pallas_call(
        pack_kernel,
        out_shape=(
            jax.ShapeDtypeStruct((2, 4, 4, 2, 2, 2, BLK, BLK), BF16),
            jax.ShapeDtypeStruct((2, 9), jnp.int32),
            jax.ShapeDtypeStruct((2, 18), jnp.int32),
        ),
        in_specs=[pl.BlockSpec(memory_space=pltpu.SMEM), pl.BlockSpec(memory_space=pl.ANY)],
        out_specs=(
            pl.BlockSpec(memory_space=pl.ANY),
            pl.BlockSpec(memory_space=pltpu.SMEM),
            pl.BlockSpec(memory_space=pltpu.SMEM),
        ),
        scratch_shapes=[
            pltpu.VMEM((8, 2, BLK, 16 * BLK), BF16),
            pltpu.VMEM((2, 4, 4, 2, 2, 2, BLK, BLK), BF16),
            pltpu.SMEM((2, 8), jnp.int32),
            pltpu.SMEM((2, 16), jnp.int32),
            pltpu.SemaphoreType.DMA((8,)),
            pltpu.SemaphoreType.DMA((1,)),
        ],
        compiler_params=pltpu.CompilerParams(vmem_limit_bytes=60 << 20),
        name="pack",
    )(child_maps, children)


def identity():
    r = lax.broadcasted_iota(jnp.int32, (BLK, BLK), 0)
    k = lax.broadcasted_iota(jnp.int32, (BLK, BLK), 1)
    return jnp.where(r == k, 1.0, 0.0).astype(BF16)


def place(row, col):
    return col // 2 * 2 + row % 2, row // 2, col % 2


def device(x, z, core):
    return {"row": z * 2 + x % 2, "col": x // 2 * 2 + core}


def ring(t):
    t = (t + 4) % 4
    return t - 2 * (t // 3)


def apart(x, z, tx, tz):
    return ring(tx - x) + ring(tz - z)


def wants(x, z, core, tx, tz, half):
    a, b = z * 2 + x % 2, x // 2 * 2 + core
    alpha = b + 4 * half
    ox, oz, _ = place(alpha, a % 4)
    here, there = apart(x, z, tx, tz), apart(ox, oz, tx, tz)
    return here <= there, here < there


def unit(packed, x, z, core, tx, tz, tcore, half, kind, h):
    a, b = z * 2 + x % 2, x // 2 * 2 + core
    alpha = b + 4 * half
    d, e = tz * 2 + tx % 2, tx // 2 * 2 + tcore
    if kind == 0:
        return packed.at[half, d % 4, e, d // 4, h], a * 8 + b * 2 + half
    return packed.at[half, e, d % 4, h, d // 4], alpha * 8 + a % 4 * 2 + a // 4


def far_step(n):
    k = n % 3
    return 2 - k + 3 * (k // 2), 1 + n // 6, n // 3 % 2


def near_step(n):
    dx = (1 - n // 6) * (1 - n // 12) * (n // 2 + 1)
    dz = n // 6 * (1 - n // 12) * ((n - 6) // 2 + 1)
    return dx, dz, n % 2 * (1 - n // 12) + n // 12


def greet_neighbours(barrier, x, z, core):
    def greet(n, carry):
        dx, dz, dc = near_step(n)
        pl.semaphore_signal(
            barrier, inc=1, device_id=device((x + dx) % 4, (z + dz) % 4, (core + dc) % 2),
            device_id_type=pl.DeviceIdType.MESH,
        )
        return carry

    lax.fori_loop(0, 13, greet, 0)
    pl.semaphore_wait(barrier, 13)


def split(x):
    hi = x.astype(BF16)
    lo = (x - hi.astype(F32)).astype(BF16)
    return hi, lo


def pieces(x):
    a = x.astype(BF16).astype(F32)
    b = (x - a).astype(BF16).astype(F32)
    return a, b, x - a - b


def factor_rows(r, mat, base):
    span = pl.ds(base, 3 * BLK)
    lane = lax.broadcasted_iota(jnp.int32, (8, 2 * BLK - base), 1) + base
    wide = lax.broadcasted_iota(jnp.int32, (8, 3 * BLK), 1) + base
    sub = lax.broadcasted_iota(jnp.int32, (8, 1), 0)
    rows = pl.ds(pl.multiple_of(r * 8, 8), 8)
    w = mat[rows, span]
    head = w[:, : 2 * BLK - base]
    col = [jnp.sum(jnp.where(lane == r * 8 + j, head, 0.0), axis=1, keepdims=True) for j in range(8)]
    for j in range(8):
        pivot = col[j][j : j + 1]
        inv = lax.rsqrt(pivot)
        inv = inv * (1.5 - 0.5 * pivot * inv * inv)
        mult = jnp.where(sub > j, col[j] * inv, 0.0)
        for k in range(j + 1, 8):
            col[k] = col[k] - mult * (col[k][j : j + 1] * inv)
        top = w[j : j + 1] * inv
        w = jnp.where(sub == j, top, w - mult * top)
    w = jnp.where(wide < r * 8 + sub, 0.0, w)
    mat[rows, span] = w
    a, b, c = pieces(w)
    u = [part[:, : 2 * BLK - base] for part in (a, a, b, a, c, b)]
    left = jnp.concatenate(u, axis=0).astype(BF16)
    right = jnp.concatenate([a, b, a, c, a, b], axis=0).astype(BF16)
    update = lax.dot_general(left, right, (((0,), (0,)), ((), ())), preferred_element_type=F32)
    below = lax.broadcasted_iota(jnp.int32, (2 * BLK - base, 1), 0) + base >= (r + 1) * 8
    rest = pl.ds(base, 2 * BLK - base)
    mat[rest, span] = mat[rest, span] - jnp.where(below, update, 0.0)


def front_kernel(
    row_tab, col_tab, packed, front, out_a, out_b, rows_out, cols_out,
    recv_a, recv_b, hold, mine, rows, cols, column, corner, mat, rows_sol, cols_sol, inv,
    send_sem, recv_sem, hold_sem, row_sem, column_sem, col_sem, corner_sem, out_sem,
):
    x, z, core = place(lax.axis_index("row"), lax.axis_index("col"))
    owner = x < 2
    root = x // 2 == z % 2
    other = 1 - core
    side = x + 1 - x % 2 * 2
    recv = (recv_a, recv_b)
    start = lambda copy: copy.start()
    done = lambda copy: copy.wait_send()

    def remote(src, dst, arrived, tx, tz, tcore):
        return pltpu.make_async_remote_copy(
            src_ref=src, dst_ref=dst, send_sem=send_sem, recv_sem=arrived,
            device_id=device(tx, tz, tcore), device_id_type=pl.DeviceIdType.MESH,
        )

    def arrive(ref, sem):
        pltpu.make_async_copy(ref, ref, sem).wait()

    def loop(lo, hi, body):
        def step(n, carry):
            body(n)
            return carry

        lax.fori_loop(lo, hi, step, 0)

    def each(sx, sz, tx, tz, fn):
        for half in range(2):
            for kind, wanted in enumerate(wants(sx, sz, core, tx, tz, half)):
                for h in range(2):

                    @pl.when(wanted)
                    def _():
                        fn(half, kind, h)

    def far(n, act):
        dz, dx, dc = far_step(n)
        tx, tz, tcore = (x + dx) % 4, (z + dz) % 4, (core + dc) % 2

        def one(half, kind, h):
            src, _ = unit(packed, x, z, core, tx, tz, tcore, half, kind, h)
            slot = n * 4 + half * 2 + kind
            act(remote(src, hold.at[slot, h], hold_sem.at[slot, h], x, tz, core))

        each(x, z, tx, tz, one)

    def near(n, act):
        dx, dz, dc = near_step(n)
        tx, tz, tcore = (x + dx) % 4, (z + dz) % 4, (core + dc) % 2

        def one(half, kind, h):
            src, dst = unit(packed, x, z, core, tx, tz, tcore, half, kind, h)
            act(remote(src, recv[h].at[dst], recv_sem.at[dst, h], tx, tz, tcore))

        each(x, z, tx, tz, one)

    def own():
        def one(half, kind, h):
            src, dst = unit(packed, x, z, core, x, z, core, half, kind, h)
            pltpu.make_async_copy(src, recv[h].at[dst], recv_sem.at[dst, h]).start()

        each(x, z, x, z, one)

    def pass_on(n, act, wait):
        dz, dx, dc = far_step(n)
        sz = (z - dz + 4) % 4
        tx, tcore = (x + dx) % 4, (core + dc) % 2

        def one(half, kind, h):
            _, dst = unit(packed, x, sz, core, tx, z, tcore, half, kind, h)
            slot = n * 4 + half * 2 + kind
            if wait:
                arrive(hold.at[slot, h], hold_sem.at[slot, h])
            act(remote(hold.at[slot, h], recv[h].at[dst], recv_sem.at[dst, h], tx, z, tcore))

        each(x, sz, tx, z, one)

    def settle(slot, halves):
        for h in halves:
            arrive(recv[h].at[slot], recv_sem.at[slot, h])
        row, u = slot // 8, slot % 8
        alpha = u // 2 + u % 2 * 4
        nx, nz, _ = place(row, alpha % 4)
        ox, oz, _ = place(alpha, row % 4)

        @pl.when(apart(ox, oz, x, z) < apart(nx, nz, x, z))
        def _():
            turned = [
                lax.dot_general(
                    identity(), recv[h][slot].reshape(2 * BLK, BLK), (((1,), (1,)), ((), ())),
                    preferred_element_type=F32,
                ).astype(BF16)
                for h in halves
            ]
            for h, both in zip(halves, turned):
                for c in range(2):
                    recv[h][slot, c] = both[:, c * BLK : (c + 1) * BLK]

    def corner_out(act):
        @pl.when(owner & (z == 0))
        def _():
            for dz in range(1, 4):
                act(remote(mine.at[0], corner.at[x, core], corner_sem.at[x, core], x, (z + dz) % 4, core))

    def corner_across(act):
        @pl.when(owner)
        def _():
            for dx in range(1, 4):
                act(
                    remote(
                        corner.at[x, core], corner.at[x, core], corner_sem.at[x, core], (x + dx) % 4, z, core
                    )
                )

    def corner_swap(v, act):
        act(remote(corner.at[v, core], corner.at[v, core], corner_sem.at[v, core], x, z, other))

    def row_out(s, act):
        @pl.when(owner)
        def _():
            act(remote(mine.at[s], rows.at[core, s], row_sem.at[core, s], (x + 2) % 4, z, core))

    def row_swap(s, act):
        act(remote(rows.at[core, s], rows.at[core, s], row_sem.at[core, s], x, z, other))

    def down_column(s, act):
        @pl.when(root)
        def _():
            for dz in range(1, 4):
                act(
                    remote(
                        rows.at[core, s], column.at[z // 2, s], column_sem.at[z // 2, s], x, (z + dz) % 4, core
                    )
                )

    def to_side(n, act):
        h, s = n % 2, n // 2
        act(remote(column.at[h, s], cols.at[h, core, s], col_sem.at[h, core, s], side, z, x % 2))

        @pl.when(core != x % 2)
        def _():
            act(remote(column.at[h, s], cols.at[h, core, s], col_sem.at[h, core, s], x, z, other))

    barrier = pltpu.get_barrier_semaphore()
    greet_neighbours(barrier, x, z, core)

    loop(0, 6, lambda n: near(n, start))
    loop(0, 18, lambda n: far(n, start))
    loop(6, 13, lambda n: near(n, start))
    own()
    loop(0, 18, lambda n: pass_on(n, start, True))
    @pl.when(owner)
    def _():
        loop(0, 64, lambda slot: settle(slot, (0,)))
        for s in range(9):
            total = front[pl.ds(s * BLK, BLK), :].astype(F32)
            for c in range(2):
                row, u = row_tab[c, s], col_tab[c, 0]
                blk = recv_a[jnp.maximum(row, 0) * 8 + jnp.maximum(u, 0), c].astype(F32)
                total += jnp.where((row >= 0) & (u >= 0), blk, 0.0)
            mine[s] = total

    corner_out(start)

    @pl.when(owner & (z == 0))
    def _():
        pltpu.make_async_copy(mine.at[0], corner.at[x, core], corner_sem.at[x, core]).start()

    def first(s):
        row_out(s, start)

        @pl.when(owner)
        def _():
            pltpu.make_async_copy(mine.at[s], rows.at[core, s], row_sem.at[core, s]).start()

    loop(0, 9, first)

    def second(s):
        arrive(rows.at[core, s], row_sem.at[core, s])
        row_swap(s, start)
        down_column(s, start)

        @pl.when(root)
        def _():
            pltpu.make_async_copy(rows.at[core, s], column.at[z // 2, s], column_sem.at[z // 2, s]).start()

    @pl.when(jnp.logical_not(owner))
    def _():
        loop(0, 64, lambda slot: settle(slot, (0, 1)))

    loop(0, 9, second)

    @pl.when(owner)
    def _():
        loop(0, 64, lambda slot: settle(slot, (1,)))

    outs = [
        pltpu.make_async_copy(recv_a, out_a, out_sem.at[0]),
        pltpu.make_async_copy(recv_b, out_b, out_sem.at[1]),
    ]
    for copy in outs:
        copy.start()

    @pl.when(owner)
    def _():
        arrive(corner.at[x, core], corner_sem.at[x, core])

    corner_across(start)

    @pl.when(x != 0)
    def _():
        arrive(corner.at[0, core], corner_sem.at[0, core])

    corner_swap(0, start)

    @pl.when(x != 1)
    def _():
        arrive(corner.at[1, core], corner_sem.at[1, core])

    corner_swap(1, start)
    for v in range(2):
        arrive(corner.at[v, other], corner_sem.at[v, other])
    r = lax.broadcasted_iota(jnp.int32, (2 * BLK, 2 * BLK), 0)
    k = lax.broadcasted_iota(jnp.int32, (2 * BLK, 2 * BLK), 1)
    mat[:, pl.ds(2 * BLK, 2 * BLK)] = jnp.where(r == k, 1.0, 0.0)
    for v in range(2):
        for p in range(2):
            mat[pl.ds(v * BLK, BLK), pl.ds(p * BLK, BLK)] = corner[v, p]

    def fourth(n):
        h, s = n % 2, n // 2
        arrive(column.at[h, s], column_sem.at[h, s])
        to_side(n, start)

        @pl.when(core == x % 2)
        def _():
            pltpu.make_async_copy(column.at[h, s], cols.at[h, core, s], col_sem.at[h, core, s]).start()

        for g in range(2):

            @pl.when((n >= g * 8) & (n < g * 8 + 8))
            def _():
                factor_rows(n * 2, mat, g * BLK)
                factor_rows(n * 2 + 1, mat, g * BLK)

    loop(0, 18, fourth)

    inv_hi, inv_lo = split(mat[:, pl.ds(2 * BLK, 2 * BLK)])
    inv[:, pl.ds(0, 2 * BLK)] = inv_hi
    inv[:, pl.ds(2 * BLK, 2 * BLK)] = inv_hi
    inv[:, pl.ds(4 * BLK, 2 * BLK)] = inv_lo

    def solve(left, right):
        pair = jnp.concatenate([left.reshape(3 * BLK, BLK), right.reshape(3 * BLK, BLK)], axis=1)
        hi, lo = split(pair)
        return lax.dot_general(
            jnp.concatenate([hi, lo, hi], axis=1), inv[...], (((1,), (1,)), ((), ())), preferred_element_type=F32
        )

    def solve_row(i):
        for j in range(3):
            arrive(rows.at[other, i * 3 + j], row_sem.at[other, i * 3 + j])
        three = pl.ds(i * 3, 3)
        rows_sol[three] = solve(rows[0, three], rows[1, three]).reshape(3, BLK, 2 * BLK)

    loop(0, 3, solve_row)

    outs.append(pltpu.make_async_copy(rows_sol, rows_out, out_sem.at[2]))
    outs[2].start()

    def solve_col(n):
        h, i = n % 2, n // 2
        for p in range(2):
            for j in range(3):
                arrive(cols.at[h, p, i * 3 + j], col_sem.at[h, p, i * 3 + j])
        three = pl.ds(i * 3, 3)
        hi, lo = split(solve(cols[h, 0, three], cols[h, 1, three]).reshape(3, BLK, 2 * BLK))
        cols_sol[h, three, :, pl.ds(0, 2 * BLK)] = hi
        cols_sol[h, three, :, pl.ds(2 * BLK, 2 * BLK)] = lo

    loop(0, 6, solve_col)
    last = pltpu.make_async_copy(cols_sol, cols_out, out_sem.at[3])
    last.start()

    def finish(n):
        far(n, done)
        pass_on(n, done, False)

        @pl.when(n < 13)
        def _():
            near(n, done)

        to_side(n, done)

        @pl.when(n < 9)
        def _():
            row_out(n, done)
            row_swap(n, done)
            down_column(n, done)

    loop(0, 18, finish)
    corner_out(done)
    corner_across(done)
    for v in range(2):
        corner_swap(v, done)
    for copy in outs:
        copy.wait()
    last.wait()


def front_stage(row_tab, col_tab, packed, front):
    anywhere = pl.BlockSpec(memory_space=pl.ANY)
    return pl.pallas_call(
        front_kernel,
        grid=(1,),
        out_shape=(
            jax.ShapeDtypeStruct((64, 2, BLK, BLK), BF16),
            jax.ShapeDtypeStruct((64, 2, BLK, BLK), BF16),
            jax.ShapeDtypeStruct((9, BLK, 2 * BLK), F32),
            jax.ShapeDtypeStruct((2, 9, BLK, 4 * BLK), BF16),
        ),
        in_specs=[
            pl.BlockSpec(memory_space=pltpu.SMEM),
            pl.BlockSpec(memory_space=pltpu.SMEM),
            anywhere,
            pl.BlockSpec((9 * BLK, BLK), lambda i: (0, 0)),
        ],
        out_specs=(anywhere, anywhere, anywhere, anywhere),
        scratch_shapes=[
            pltpu.VMEM((64, 2, BLK, BLK), BF16),
            pltpu.VMEM((64, 2, BLK, BLK), BF16),
            pltpu.VMEM((72, 2, 2, BLK, BLK), BF16),
            pltpu.VMEM((9, BLK, BLK), F32),
            pltpu.VMEM((2, 9, BLK, BLK), F32),
            pltpu.VMEM((2, 2, 9, BLK, BLK), F32),
            pltpu.VMEM((2, 9, BLK, BLK), F32),
            pltpu.VMEM((2, 2, BLK, BLK), F32),
            pltpu.VMEM((2 * BLK, 4 * BLK), F32),
            pltpu.VMEM((9, BLK, 2 * BLK), F32),
            pltpu.VMEM((2, 9, BLK, 4 * BLK), BF16),
            pltpu.VMEM((2 * BLK, 6 * BLK), BF16),
            pltpu.SemaphoreType.DMA(()),
            pltpu.SemaphoreType.DMA((64, 2)),
            pltpu.SemaphoreType.DMA((72, 2)),
            pltpu.SemaphoreType.DMA((2, 9)),
            pltpu.SemaphoreType.DMA((2, 9)),
            pltpu.SemaphoreType.DMA((2, 2, 9)),
            pltpu.SemaphoreType.DMA((2, 2)),
            pltpu.SemaphoreType.DMA((4,)),
        ],
        compiler_params=pltpu.CompilerParams(
            collective_id=0, has_side_effects=True, vmem_limit_bytes=62 << 20
        ),
        name="front_stage",
    )(row_tab, col_tab, packed, front)


def final_kernel(row_tab, col_tab, *refs):
    recv = [refs[4 * j : 4 * j + 4] for j in range(3)]
    front, rows, cols, out = refs[12:]
    step = pl.program_id(0)
    own_row, own_col = lax.axis_index("row"), lax.axis_index("col")
    hi, lo = split(rows[...].reshape(3 * BLK, 2 * BLK))
    left = jnp.concatenate([hi, lo, hi], axis=1)
    for t in range(18):
        part = pl.ds(t * BLK, BLK)
        right = jnp.concatenate([cols[t % 2, t // 2, :, pl.ds(k, 256)] for k in (0, 0, 256)], axis=1)
        val = front[:, part].astype(F32) - lax.dot_general(
            left, right, (((1,), (1,)), ((), ())), preferred_element_type=F32
        )
        for j in range(3):
            here = val[j * BLK : (j + 1) * BLK]
            for c in range(2):
                u = col_tab[c, t]
                blk = recv[j][c * 2 + t % 2][0, jnp.maximum(u, 0), 0].astype(F32)
                here += jnp.where((u >= 0) & (row_tab[c, step * 3 + j] >= 0), blk, 0.0)
            out[pl.ds(j * BLK, BLK), part] = here

    @pl.when(own_col < 2)
    def _():
        for j in range(3):
            out[pl.ds(j * BLK, BLK), pl.ds(0, BLK)] = jnp.where(
                own_col == 0, rows[j, :, pl.ds(0, BLK)], rows[j, :, pl.ds(BLK, BLK)]
            )

    @pl.when((step == 0) & (own_row < 2))
    def _():
        out[pl.ds(0, BLK), :] = jnp.zeros((BLK, 18 * BLK), F32)

        @pl.when(own_col < 2)
        def _():
            r = lax.broadcasted_iota(jnp.int32, (BLK, BLK), 0) + own_row * BLK
            k = lax.broadcasted_iota(jnp.int32, (BLK, BLK), 1) + own_col * BLK
            mine = jnp.where(own_col == 0, rows[0, :, pl.ds(0, BLK)], rows[0, :, pl.ds(BLK, BLK)])
            out[pl.ds(0, BLK), pl.ds(0, BLK)] = jnp.where(r >= k, mine, 0.0)


def final(row_tab, col_tab, recv_a, recv_b, front, rows, cols):
    def recv_spec(j, c):
        return pl.BlockSpec(
            (1, 8, 1, BLK, BLK),
            lambda step, row_tab, col_tab: (jnp.maximum(row_tab[c, step * 3 + j], 0), 0, c, 0, 0),
        )

    return pl.pallas_call(
        final_kernel,
        out_shape=jax.ShapeDtypeStruct((9 * BLK, 18 * BLK), F32),
        grid_spec=pltpu.PrefetchScalarGridSpec(
            num_scalar_prefetch=2,
            grid=(3,),
            in_specs=[recv_spec(j, c) for j in range(3) for c in range(2) for _ in range(2)]
            + [
                pl.BlockSpec((3 * BLK, 18 * BLK), lambda s, *_: (s, 0)),
                pl.BlockSpec((3, BLK, 2 * BLK), lambda s, *_: (s, 0, 0)),
                pl.BlockSpec((2, 9, BLK, 4 * BLK), lambda s, *_: (0, 0, 0, 0)),
            ],
            out_specs=pl.BlockSpec((3 * BLK, 18 * BLK), lambda s, *_: (s, 0)),
        ),
        compiler_params=pltpu.CompilerParams(vmem_limit_bytes=60 << 20),
        name="final",
    )(row_tab, col_tab, *([recv_a, recv_b] * 6), front, rows, cols)


def shards(front_entries, children, child_maps):
    packed, row_tab, col_tab = pack(children, child_maps)
    recv_a, recv_b, rows, cols = front_stage(row_tab, col_tab, packed, front_entries)
    recv_a, recv_b = (part.reshape(8, 8, 2, BLK, BLK) for part in (recv_a, recv_b))
    return final(row_tab, col_tab, recv_a, recv_b, front_entries, rows, cols)


def solution(mesh):
    in_specs = (P(("front", "row"), "col"), P("front", "row", "col"), P("front", None))
    out_specs = P(("front", "row"), "col")
    return jax.shard_map(shards, mesh=mesh, in_specs=in_specs, out_specs=out_specs, check_vma=False)
```

```python
import jax
import jax.numpy as jnp
from jax import lax
from jax.experimental import pallas as pl
from jax.experimental.pallas import tpu as pltpu
from jax.sharding import PartitionSpec as P

BLK = 128
F32 = jnp.float32
BF16 = jnp.bfloat16
HIGH = lax.Precision.HIGHEST


def pack_kernel(maps, children, out, rows_of, cols_of, buf, packed, row_of, col_of, in_sem, out_sem):
    own_row, own_col = lax.axis_index("row"), lax.axis_index("col")
    for c in range(2):
        for k in range(8):
            row_of[c, maps[c, k * 8 + own_row] & 7] = k
        for k in range(16):
            col_of[c, (k % 2) * 8 + (maps[c, k * 4 + own_col] & 7)] = k
    for d in range(8):
        for c in range(2):
            pltpu.make_async_copy(
                children.at[c, pl.ds(row_of[c, d] * BLK, BLK), :], buf.at[d, c], in_sem.at[d]
            ).start()
    for c in range(2):
        for s in range(9):
            rows_of[c, s] = -1
        for t in range(18):
            cols_of[c, t] = -1

        for k in range(64):
            v = maps[c, k]

            @pl.when((v & 7) == own_row)
            def _():
                rows_of[c, v >> 3] = k % 8

            @pl.when((v & 3) == own_col)
            def _():
                cols_of[c, v >> 2] = k % 4 * 2 + k % 8 // 4

    def one_row(d, carry):
        for c in range(2):
            pltpu.make_async_copy(children.at[0, pl.ds(0, BLK), :], buf.at[d, c], in_sem.at[d]).wait()
        for c in range(2):
            for half in range(2):
                for delta in range(8):
                    start = pl.multiple_of(col_of[c, half * 8 + delta] * BLK, BLK)
                    packed[half, d % 4, delta % 4, d // 4, delta // 4, c] = buf[d, c, :, pl.ds(start, BLK)]
        pltpu.make_async_copy(
            packed.at[:, d % 4, :, d // 4], out.at[:, d % 4, :, d // 4], out_sem.at[0]
        ).start()
        return carry

    lax.fori_loop(0, 8, one_row, 0)
    pltpu.make_async_copy(packed, out, out_sem.at[0]).wait()


def pack(children, child_maps):
    return pl.pallas_call(
        pack_kernel,
        out_shape=(
            jax.ShapeDtypeStruct((2, 4, 4, 2, 2, 2, BLK, BLK), BF16),
            jax.ShapeDtypeStruct((2, 9), jnp.int32),
            jax.ShapeDtypeStruct((2, 18), jnp.int32),
        ),
        in_specs=[pl.BlockSpec(memory_space=pltpu.SMEM), pl.BlockSpec(memory_space=pl.ANY)],
        out_specs=(
            pl.BlockSpec(memory_space=pl.ANY),
            pl.BlockSpec(memory_space=pltpu.SMEM),
            pl.BlockSpec(memory_space=pltpu.SMEM),
        ),
        scratch_shapes=[
            pltpu.VMEM((8, 2, BLK, 16 * BLK), BF16),
            pltpu.VMEM((2, 4, 4, 2, 2, 2, BLK, BLK), BF16),
            pltpu.SMEM((2, 8), jnp.int32),
            pltpu.SMEM((2, 16), jnp.int32),
            pltpu.SemaphoreType.DMA((8,)),
            pltpu.SemaphoreType.DMA((1,)),
        ],
        compiler_params=pltpu.CompilerParams(vmem_limit_bytes=60 << 20),
        name="pack",
    )(child_maps, children)


def identity():
    r = lax.broadcasted_iota(jnp.int32, (BLK, BLK), 0)
    k = lax.broadcasted_iota(jnp.int32, (BLK, BLK), 1)
    return jnp.where(r == k, 1.0, 0.0).astype(BF16)


def place(row, col):
    return col // 2 * 2 + row % 2, row // 2, col % 2


def device(x, z, core):
    return {"row": z * 2 + x % 2, "col": x // 2 * 2 + core}


def ring(t):
    t = (t + 4) % 4
    return t - 2 * (t // 3)


def apart(x, z, tx, tz):
    return ring(tx - x) + ring(tz - z)


def wants(x, z, core, tx, tz, half):
    a, b = z * 2 + x % 2, x // 2 * 2 + core
    alpha = b + 4 * half
    ox, oz, _ = place(alpha, a % 4)
    here, there = apart(x, z, tx, tz), apart(ox, oz, tx, tz)
    return here <= there, here < there


def unit(packed, x, z, core, tx, tz, tcore, half, kind, h):
    a, b = z * 2 + x % 2, x // 2 * 2 + core
    alpha = b + 4 * half
    d, e = tz * 2 + tx % 2, tx // 2 * 2 + tcore
    if kind == 0:
        return packed.at[half, d % 4, e, d // 4, h], a * 8 + b * 2 + half
    return packed.at[half, e, d % 4, h, d // 4], alpha * 8 + a % 4 * 2 + a // 4


def far_step(n):
    k = n % 3
    return 2 - k + 3 * (k // 2), 1 + n // 6, n // 3 % 2


def near_step(n):
    dx = (1 - n // 6) * (1 - n // 12) * (n // 2 + 1)
    dz = n // 6 * (1 - n // 12) * ((n - 6) // 2 + 1)
    return dx, dz, n % 2 * (1 - n // 12) + n // 12


def greet_neighbours(barrier, x, z, core):
    def greet(n, carry):
        dx, dz, dc = near_step(n)
        pl.semaphore_signal(
            barrier, inc=1, device_id=device((x + dx) % 4, (z + dz) % 4, (core + dc) % 2),
            device_id_type=pl.DeviceIdType.MESH,
        )
        return carry

    lax.fori_loop(0, 13, greet, 0)
    pl.semaphore_wait(barrier, 13)


def split(x):
    hi = x.astype(BF16)
    lo = (x - hi.astype(F32)).astype(BF16)
    return hi, lo


def pieces(x):
    a = x.astype(BF16).astype(F32)
    b = (x - a).astype(BF16).astype(F32)
    return a, b, x - a - b


def factor_rows(r, mat, base):
    span = pl.ds(base, 3 * BLK)
    lane = lax.broadcasted_iota(jnp.int32, (8, 2 * BLK - base), 1) + base
    wide = lax.broadcasted_iota(jnp.int32, (8, 3 * BLK), 1) + base
    sub = lax.broadcasted_iota(jnp.int32, (8, 1), 0)
    rows = pl.ds(pl.multiple_of(r * 8, 8), 8)
    w = mat[rows, span]
    head = w[:, : 2 * BLK - base]
    col = [jnp.sum(jnp.where(lane == r * 8 + j, head, 0.0), axis=1, keepdims=True) for j in range(8)]
    for j in range(8):
        pivot = col[j][j : j + 1]
        inv = lax.rsqrt(pivot)
        inv = inv * (1.5 - 0.5 * pivot * inv * inv)
        mult = jnp.where(sub > j, col[j] * inv, 0.0)
        for k in range(j + 1, 8):
            col[k] = col[k] - mult * (col[k][j : j + 1] * inv)
        top = w[j : j + 1] * inv
        w = jnp.where(sub == j, top, w - mult * top)
    w = jnp.where(wide < r * 8 + sub, 0.0, w)
    mat[rows, span] = w
    a, b, c = pieces(w)
    u = [part[:, : 2 * BLK - base] for part in (a, a, b, a, c, b)]
    left = jnp.concatenate(u, axis=0).astype(BF16)
    right = jnp.concatenate([a, b, a, c, a, b], axis=0).astype(BF16)
    update = lax.dot_general(left, right, (((0,), (0,)), ((), ())), preferred_element_type=F32)
    below = lax.broadcasted_iota(jnp.int32, (2 * BLK - base, 1), 0) + base >= (r + 1) * 8
    rest = pl.ds(base, 2 * BLK - base)
    mat[rest, span] = mat[rest, span] - jnp.where(below, update, 0.0)


def front_kernel(
    row_tab, col_tab, packed, front, out_a, out_b, rows_out, cols_out,
    recv_a, recv_b, hold, mine, rows, cols, column, corner, mat, rows_sol, cols_sol, inv,
    send_sem, recv_sem, hold_sem, row_sem, column_sem, col_sem, corner_sem, out_sem,
):
    x, z, core = place(lax.axis_index("row"), lax.axis_index("col"))
    owner = x < 2
    root = x // 2 == z % 2
    other = 1 - core
    side = x + 1 - x % 2 * 2
    recv = (recv_a, recv_b)
    start = lambda copy: copy.start()
    done = lambda copy: copy.wait_send()

    def remote(src, dst, arrived, tx, tz, tcore):
        return pltpu.make_async_remote_copy(
            src_ref=src, dst_ref=dst, send_sem=send_sem, recv_sem=arrived,
            device_id=device(tx, tz, tcore), device_id_type=pl.DeviceIdType.MESH,
        )

    def arrive(ref, sem):
        pltpu.make_async_copy(ref, ref, sem).wait()

    def loop(lo, hi, body):
        def step(n, carry):
            body(n)
            return carry

        lax.fori_loop(lo, hi, step, 0)

    def each(sx, sz, tx, tz, fn):
        for half in range(2):
            for kind, wanted in enumerate(wants(sx, sz, core, tx, tz, half)):
                for h in range(2):

                    @pl.when(wanted)
                    def _():
                        fn(half, kind, h)

    def far(n, act):
        dz, dx, dc = far_step(n)
        tx, tz, tcore = (x + dx) % 4, (z + dz) % 4, (core + dc) % 2

        def one(half, kind, h):
            src, _ = unit(packed, x, z, core, tx, tz, tcore, half, kind, h)
            slot = n * 4 + half * 2 + kind
            act(remote(src, hold.at[slot, h], hold_sem.at[slot, h], x, tz, core))

        each(x, z, tx, tz, one)

    def near(n, act):
        dx, dz, dc = near_step(n)
        tx, tz, tcore = (x + dx) % 4, (z + dz) % 4, (core + dc) % 2

        def one(half, kind, h):
            src, dst = unit(packed, x, z, core, tx, tz, tcore, half, kind, h)
            act(remote(src, recv[h].at[dst], recv_sem.at[dst, h], tx, tz, tcore))

        each(x, z, tx, tz, one)

    def own():
        def one(half, kind, h):
            src, dst = unit(packed, x, z, core, x, z, core, half, kind, h)
            pltpu.make_async_copy(src, recv[h].at[dst], recv_sem.at[dst, h]).start()

        each(x, z, x, z, one)

    def pass_on(n, act, wait):
        dz, dx, dc = far_step(n)
        sz = (z - dz + 4) % 4
        tx, tcore = (x + dx) % 4, (core + dc) % 2

        def one(half, kind, h):
            _, dst = unit(packed, x, sz, core, tx, z, tcore, half, kind, h)
            slot = n * 4 + half * 2 + kind
            if wait:
                arrive(hold.at[slot, h], hold_sem.at[slot, h])
            act(remote(hold.at[slot, h], recv[h].at[dst], recv_sem.at[dst, h], tx, z, tcore))

        each(x, sz, tx, z, one)

    def settle(slot, halves):
        for h in halves:
            arrive(recv[h].at[slot], recv_sem.at[slot, h])
        row, u = slot // 8, slot % 8
        alpha = u // 2 + u % 2 * 4
        nx, nz, _ = place(row, alpha % 4)
        ox, oz, _ = place(alpha, row % 4)

        @pl.when(apart(ox, oz, x, z) < apart(nx, nz, x, z))
        def _():
            turned = [
                lax.dot_general(
                    identity(), recv[h][slot].reshape(2 * BLK, BLK), (((1,), (1,)), ((), ())),
                    preferred_element_type=F32,
                ).astype(BF16)
                for h in halves
            ]
            for h, both in zip(halves, turned):
                for c in range(2):
                    recv[h][slot, c] = both[:, c * BLK : (c + 1) * BLK]

    def corner_out(act):
        @pl.when(owner & (z == 0))
        def _():
            for dz in range(1, 4):
                act(remote(mine.at[0], corner.at[x, core], corner_sem.at[x, core], x, (z + dz) % 4, core))

    def corner_across(act):
        @pl.when(owner)
        def _():
            for dx in range(1, 4):
                act(
                    remote(
                        corner.at[x, core], corner.at[x, core], corner_sem.at[x, core], (x + dx) % 4, z, core
                    )
                )

    def corner_swap(v, act):
        act(remote(corner.at[v, core], corner.at[v, core], corner_sem.at[v, core], x, z, other))

    def row_out(s, act):
        @pl.when(owner)
        def _():
            act(remote(mine.at[s], rows.at[core, s], row_sem.at[core, s], (x + 2) % 4, z, core))

    def row_swap(s, act):
        act(remote(rows.at[core, s], rows.at[core, s], row_sem.at[core, s], x, z, other))

    def down_column(s, act):
        @pl.when(root)
        def _():
            for dz in range(1, 4):
                act(
                    remote(
                        rows.at[core, s], column.at[z // 2, s], column_sem.at[z // 2, s], x, (z + dz) % 4, core
                    )
                )

    def to_side(n, act):
        h, s = n % 2, n // 2
        act(remote(column.at[h, s], cols.at[h, core, s], col_sem.at[h, core, s], side, z, x % 2))

        @pl.when(core != x % 2)
        def _():
            act(remote(column.at[h, s], cols.at[h, core, s], col_sem.at[h, core, s], x, z, other))

    barrier = pltpu.get_barrier_semaphore()
    greet_neighbours(barrier, x, z, core)

    loop(0, 6, lambda n: near(n, start))
    loop(0, 18, lambda n: far(n, start))
    loop(6, 13, lambda n: near(n, start))
    own()
    loop(0, 18, lambda n: pass_on(n, start, True))
    @pl.when(owner)
    def _():
        loop(0, 64, lambda slot: settle(slot, (0,)))
        for s in range(9):
            total = front[pl.ds(s * BLK, BLK), :].astype(F32)
            for c in range(2):
                row, u = row_tab[c, s], col_tab[c, 0]
                blk = recv_a[jnp.maximum(row, 0) * 8 + jnp.maximum(u, 0), c].astype(F32)
                total += jnp.where((row >= 0) & (u >= 0), blk, 0.0)
            mine[s] = total

    corner_out(start)

    @pl.when(owner & (z == 0))
    def _():
        pltpu.make_async_copy(mine.at[0], corner.at[x, core], corner_sem.at[x, core]).start()

    def first(s):
        row_out(s, start)

        @pl.when(owner)
        def _():
            pltpu.make_async_copy(mine.at[s], rows.at[core, s], row_sem.at[core, s]).start()

    loop(0, 9, first)

    def second(s):
        arrive(rows.at[core, s], row_sem.at[core, s])
        row_swap(s, start)
        down_column(s, start)

        @pl.when(root)
        def _():
            pltpu.make_async_copy(rows.at[core, s], column.at[z // 2, s], column_sem.at[z // 2, s]).start()

    @pl.when(jnp.logical_not(owner))
    def _():
        loop(0, 64, lambda slot: settle(slot, (0, 1)))

    loop(0, 9, second)

    @pl.when(owner)
    def _():
        loop(0, 64, lambda slot: settle(slot, (1,)))

    outs = [
        pltpu.make_async_copy(recv_a, out_a, out_sem.at[0]),
        pltpu.make_async_copy(recv_b, out_b, out_sem.at[1]),
    ]
    for copy in outs:
        copy.start()

    @pl.when(owner)
    def _():
        arrive(corner.at[x, core], corner_sem.at[x, core])

    corner_across(start)

    @pl.when(x != 0)
    def _():
        arrive(corner.at[0, core], corner_sem.at[0, core])

    corner_swap(0, start)

    @pl.when(x != 1)
    def _():
        arrive(corner.at[1, core], corner_sem.at[1, core])

    corner_swap(1, start)
    for v in range(2):
        arrive(corner.at[v, other], corner_sem.at[v, other])
    r = lax.broadcasted_iota(jnp.int32, (2 * BLK, 2 * BLK), 0)
    k = lax.broadcasted_iota(jnp.int32, (2 * BLK, 2 * BLK), 1)
    mat[:, pl.ds(2 * BLK, 2 * BLK)] = jnp.where(r == k, 1.0, 0.0)
    for v in range(2):
        for p in range(2):
            mat[pl.ds(v * BLK, BLK), pl.ds(p * BLK, BLK)] = corner[v, p]

    def fourth(n):
        h, s = n % 2, n // 2
        arrive(column.at[h, s], column_sem.at[h, s])
        to_side(n, start)

        @pl.when(core == x % 2)
        def _():
            pltpu.make_async_copy(column.at[h, s], cols.at[h, core, s], col_sem.at[h, core, s]).start()

        for g in range(2):

            @pl.when((n >= g * 8) & (n < g * 8 + 8))
            def _():
                factor_rows(n * 2, mat, g * BLK)
                factor_rows(n * 2 + 1, mat, g * BLK)

    loop(0, 18, fourth)

    inv_hi, inv_lo = split(mat[:, pl.ds(2 * BLK, 2 * BLK)])
    inv[:, pl.ds(0, 2 * BLK)] = inv_hi
    inv[:, pl.ds(2 * BLK, 2 * BLK)] = inv_hi
    inv[:, pl.ds(4 * BLK, 2 * BLK)] = inv_lo

    def solve(left, right):
        pair = jnp.concatenate([left.reshape(3 * BLK, BLK), right.reshape(3 * BLK, BLK)], axis=1)
        hi, lo = split(pair)
        return lax.dot_general(
            jnp.concatenate([hi, lo, hi], axis=1), inv[...], (((1,), (1,)), ((), ())), preferred_element_type=F32
        )

    def solve_row(i):
        for j in range(3):
            arrive(rows.at[other, i * 3 + j], row_sem.at[other, i * 3 + j])
        three = pl.ds(i * 3, 3)
        rows_sol[three] = solve(rows[0, three], rows[1, three]).reshape(3, BLK, 2 * BLK)

    loop(0, 3, solve_row)

    outs.append(pltpu.make_async_copy(rows_sol, rows_out, out_sem.at[2]))
    outs[2].start()

    def solve_col(n):
        h, i = n % 2, n // 2
        for p in range(2):
            for j in range(3):
                arrive(cols.at[h, p, i * 3 + j], col_sem.at[h, p, i * 3 + j])
        three = pl.ds(i * 3, 3)
        hi, lo = split(solve(cols[h, 0, three], cols[h, 1, three]).reshape(3, BLK, 2 * BLK))
        cols_sol[h, three, :, pl.ds(0, 2 * BLK)] = hi
        cols_sol[h, three, :, pl.ds(2 * BLK, 2 * BLK)] = lo

    loop(0, 6, solve_col)
    last = pltpu.make_async_copy(cols_sol, cols_out, out_sem.at[3])
    last.start()

    def finish(n):
        far(n, done)
        pass_on(n, done, False)

        @pl.when(n < 13)
        def _():
            near(n, done)

        to_side(n, done)

        @pl.when(n < 9)
        def _():
            row_out(n, done)
            row_swap(n, done)
            down_column(n, done)

    loop(0, 18, finish)
    corner_out(done)
    corner_across(done)
    for v in range(2):
        corner_swap(v, done)
    for copy in outs:
        copy.wait()
    last.wait()


def front_stage(row_tab, col_tab, packed, front):
    anywhere = pl.BlockSpec(memory_space=pl.ANY)
    return pl.pallas_call(
        front_kernel,
        grid=(1,),
        out_shape=(
            jax.ShapeDtypeStruct((64, 2, BLK, BLK), BF16),
            jax.ShapeDtypeStruct((64, 2, BLK, BLK), BF16),
            jax.ShapeDtypeStruct((9, BLK, 2 * BLK), F32),
            jax.ShapeDtypeStruct((2, 9, BLK, 4 * BLK), BF16),
        ),
        in_specs=[
            pl.BlockSpec(memory_space=pltpu.SMEM),
            pl.BlockSpec(memory_space=pltpu.SMEM),
            anywhere,
            pl.BlockSpec((9 * BLK, BLK), lambda i: (0, 0)),
        ],
        out_specs=(anywhere, anywhere, anywhere, anywhere),
        scratch_shapes=[
            pltpu.VMEM((64, 2, BLK, BLK), BF16),
            pltpu.VMEM((64, 2, BLK, BLK), BF16),
            pltpu.VMEM((72, 2, 2, BLK, BLK), BF16),
            pltpu.VMEM((9, BLK, BLK), F32),
            pltpu.VMEM((2, 9, BLK, BLK), F32),
            pltpu.VMEM((2, 2, 9, BLK, BLK), F32),
            pltpu.VMEM((2, 9, BLK, BLK), F32),
            pltpu.VMEM((2, 2, BLK, BLK), F32),
            pltpu.VMEM((2 * BLK, 4 * BLK), F32),
            pltpu.VMEM((9, BLK, 2 * BLK), F32),
            pltpu.VMEM((2, 9, BLK, 4 * BLK), BF16),
            pltpu.VMEM((2 * BLK, 6 * BLK), BF16),
            pltpu.SemaphoreType.DMA(()),
            pltpu.SemaphoreType.DMA((64, 2)),
            pltpu.SemaphoreType.DMA((72, 2)),
            pltpu.SemaphoreType.DMA((2, 9)),
            pltpu.SemaphoreType.DMA((2, 9)),
            pltpu.SemaphoreType.DMA((2, 2, 9)),
            pltpu.SemaphoreType.DMA((2, 2)),
            pltpu.SemaphoreType.DMA((4,)),
        ],
        compiler_params=pltpu.CompilerParams(
            collective_id=0, has_side_effects=True, vmem_limit_bytes=62 << 20
        ),
        name="front_stage",
    )(row_tab, col_tab, packed, front)


def final_kernel(row_tab, col_tab, *refs):
    recv = [refs[4 * j : 4 * j + 4] for j in range(3)]
    front, rows, cols, out = refs[12:]
    step = pl.program_id(0)
    own_row, own_col = lax.axis_index("row"), lax.axis_index("col")
    hi, lo = split(rows[...].reshape(3 * BLK, 2 * BLK))
    left = jnp.concatenate([hi, lo, hi], axis=1)
    for i in range(9):
        right = jnp.concatenate(
            [cols[:, i, :, pl.ds(k, 256)].reshape(2 * BLK, 2 * BLK) for k in (0, 0, 256)], axis=1
        )
        product = lax.dot_general(left, right, (((1,), (1,)), ((), ())), preferred_element_type=F32)
        for h in range(2):
            t = i * 2 + h
            part = pl.ds(t * BLK, BLK)
            for j in range(3):
                slot = pl.ds(j * BLK, BLK)
                here = front[slot, part].astype(F32) - product[j * BLK : (j + 1) * BLK, h * BLK : (h + 1) * BLK]
                for c in range(2):
                    u = col_tab[c, t]
                    blk = recv[j][c * 2 + h][0, jnp.maximum(u, 0), 0].astype(F32)
                    here += jnp.where((u >= 0) & (row_tab[c, step * 3 + j] >= 0), blk, 0.0)
                out[slot, part] = here

    @pl.when(own_col < 2)
    def _():
        for j in range(3):
            out[pl.ds(j * BLK, BLK), pl.ds(0, BLK)] = jnp.where(
                own_col == 0, rows[j, :, pl.ds(0, BLK)], rows[j, :, pl.ds(BLK, BLK)]
            )

    @pl.when((step == 0) & (own_row < 2))
    def _():
        out[pl.ds(0, BLK), :] = jnp.zeros((BLK, 18 * BLK), F32)

        @pl.when(own_col < 2)
        def _():
            r = lax.broadcasted_iota(jnp.int32, (BLK, BLK), 0) + own_row * BLK
            k = lax.broadcasted_iota(jnp.int32, (BLK, BLK), 1) + own_col * BLK
            mine = jnp.where(own_col == 0, rows[0, :, pl.ds(0, BLK)], rows[0, :, pl.ds(BLK, BLK)])
            out[pl.ds(0, BLK), pl.ds(0, BLK)] = jnp.where(r >= k, mine, 0.0)


def final(row_tab, col_tab, recv_a, recv_b, front, rows, cols):
    def recv_spec(j, c):
        return pl.BlockSpec(
            (1, 8, 1, BLK, BLK),
            lambda step, row_tab, col_tab: (jnp.maximum(row_tab[c, step * 3 + j], 0), 0, c, 0, 0),
        )

    return pl.pallas_call(
        final_kernel,
        out_shape=jax.ShapeDtypeStruct((9 * BLK, 18 * BLK), F32),
        grid_spec=pltpu.PrefetchScalarGridSpec(
            num_scalar_prefetch=2,
            grid=(3,),
            in_specs=[recv_spec(j, c) for j in range(3) for c in range(2) for _ in range(2)]
            + [
                pl.BlockSpec((3 * BLK, 18 * BLK), lambda s, *_: (s, 0)),
                pl.BlockSpec((3, BLK, 2 * BLK), lambda s, *_: (s, 0, 0)),
                pl.BlockSpec((2, 9, BLK, 4 * BLK), lambda s, *_: (0, 0, 0, 0)),
            ],
            out_specs=pl.BlockSpec((3 * BLK, 18 * BLK), lambda s, *_: (s, 0)),
        ),
        compiler_params=pltpu.CompilerParams(vmem_limit_bytes=60 << 20),
        name="final",
    )(row_tab, col_tab, *([recv_a, recv_b] * 6), front, rows, cols)


def shards(front_entries, children, child_maps):
    packed, row_tab, col_tab = pack(children, child_maps)
    recv_a, recv_b, rows, cols = front_stage(row_tab, col_tab, packed, front_entries)
    recv_a, recv_b = (part.reshape(8, 8, 2, BLK, BLK) for part in (recv_a, recv_b))
    return final(row_tab, col_tab, recv_a, recv_b, front_entries, rows, cols)


def solution(mesh):
    in_specs = (P(("front", "row"), "col"), P("front", "row", "col"), P("front", None))
    out_specs = P(("front", "row"), "col")
    return jax.shard_map(shards, mesh=mesh, in_specs=in_specs, out_specs=out_specs, check_vma=False)
```
